32 devices in a mesh: grp: 2 (over x), xy: 4 (over y, core), gz: 4 (over z).
Axes of the slice: x: 2, y: 2, z: 4, core: 2. Of those that a mesh axis runs over, the one named last changes fastest.
Arguments:
- fields: float32 [12, 16, 64, 512], P('grp', 'xy', 'gz'), parts along dimension 0, may hold values from -6 to 6
- adjoint_fields: float32 [12, 16, 64, 512], P('grp', 'xy', 'gz'), parts along dimension 0, may hold values from -6 to 6
- material_ids: int32 [16, 64, 1024], P('xy', 'gz', 'grp'), parts along dimension 2, may hold values from 0 to 3
- material_eps: float32 [4], replicated, may hold values from 1 to 12
- monitor_cells: int32 [4, 4, 2048], P('xy', 'gz', 'grp'), parts along dimension 2, may hold values from 0 to 32767
- monitor_bins: int32 [4, 4, 2048], P('xy', 'gz', 'grp'), parts along dimension 2, may hold values from 0 to 127
- source_cells: int32 [4, 4, 2048], P('xy', 'gz', 'grp'), parts along dimension 2, may hold values from 0 to 32767
- source_bins: int32 [4, 4, 2048], P('xy', 'gz', 'grp'), parts along dimension 2, may hold values from 0 to 127
- bin_weight: float32 [256], P('grp'), parts along dimension 0, may hold values from 0.5 to 2
Outputs:
- forward_out: float32 [12, 16, 64, 512], P('grp', 'xy', 'gz'), parts along dimension 0
- adjoint_out: float32 [12, 16, 64, 512], P('grp', 'xy', 'gz'), parts along dimension 0
- monitor_dft: float32 [16, 128], P('grp', ('xy', 'gz')), parts along dimension 0
The draws below stay inside these ranges and needn't reach their ends.
There are 2 independent parts, one for each index of `grp`. The reference program is written for one: setup_inputs(seed, part) draws one part's arguments, and reference() takes and returns one part's arrays. A program takes and returns all parts, laid end to end along the dimension named above; an argument that names none is the same for every part. Nothing has to cross between parts.
All inputs are finite; a program needn't handle non-finite values.
Results may differ from the reference program's by a relative error of at most 0.00011.
Values sent between devices are 32-bit elements; how exact they have to be, the bound alone decides.
No kernel may reach another device: no remote copies, remote signals or barrier semaphores. Data moves between devices by JAX's collectives and lax.ppermute only.
A program may use at most 64 MiB of HBM per device.

```python
import math
import jax
import jax.numpy as jnp
from jax import lax

CX = 4
CZ = 16
NY = 512
STEPS = 8
NFREQ = 4
NMAT = 4
MON_DEV = 1024
SRC_DEV = 1024
NX = 16
NZ = 64
BINS = 128
N_XY = 4
N_GZ = 4


def plant(entries, rng, smallest, largest):
    longest = entries.shape.index(max(entries.shape))
    spots = []
    for shift in (0, 1):
        where = [jax.random.randint(jax.random.fold_in(rng, axis), (), 0, length) for axis, length in enumerate(entries.shape)]
        where[longest] = (where[longest] + shift) % entries.shape[longest]
        spots.append(tuple(where))
    return entries.at[spots[0]].set(smallest).at[spots[1]].set(largest)


def steps_of(rng, extent, pieces, smallest, top_value):
    loudness, own = 1.0, jax.random.fold_in(rng, 6)
    for position, blocks in pieces:
        draws = jnp.exp(jax.random.uniform(jax.random.fold_in(own, position), (blocks,), jnp.float32, smallest / len(pieces), top_value / len(pieces)))
        loudness = loudness * jnp.repeat(draws, extent[position] // blocks).reshape([-1 if axis == position else 1 for axis in range(len(extent))])
    return loudness


def bell_draw(own_key, extent, spread, most, shards=(), kind=jnp.bfloat16):
    values = spread * jax.random.normal(own_key, extent, jnp.float32)
    if shards:
        values = values * steps_of(own_key, extent, shards, -0.22, 0.18)
    return jnp.clip(values, -most, most).astype(kind)


def setup_inputs(seed: int = 0, part: int = 0) -> dict:
    seeds = jax.random.split(jax.random.key(seed), 10)
    part_keys = jax.random.split(jax.random.fold_in(seeds[9], part), 10)
    fields = bell_draw(part_keys[0], (6, NX, NZ, NY), 1.0, 6.0, ((1, 4), (2, 4)), jnp.float32)
    adjoint_fields = bell_draw(part_keys[1], (6, NX, NZ, NY), 0.5, 6.0, ((1, 4), (2, 4)), jnp.float32)
    material_ids = plant(jax.random.randint(part_keys[2], (NX, NZ, NY), 0, NMAT), jax.random.fold_in(part_keys[2], 1), 0, NMAT - 1).astype(jnp.int32)
    material_eps = jnp.clip(jnp.exp(jax.random.uniform(seeds[3], (NMAT,), jnp.float32, math.log(1.0), math.log(12.0))), 1.0, 12.0)
    monitor_cells = plant(jax.random.randint(part_keys[4], (N_XY, N_GZ, MON_DEV), 0, CX * CZ * NY), jax.random.fold_in(part_keys[4], 1), 0, (CX * CZ * NY) - 1).astype(jnp.int32)
    monitor_bins = plant(jax.random.randint(part_keys[5], (N_XY, N_GZ, MON_DEV), 0, BINS), jax.random.fold_in(part_keys[5], 1), 0, BINS - 1).astype(jnp.int32)
    source_cells = plant(jax.random.randint(part_keys[6], (N_XY, N_GZ, SRC_DEV), 0, CX * CZ * NY), jax.random.fold_in(part_keys[6], 1), 0, (CX * CZ * NY) - 1).astype(jnp.int32)
    source_bins = plant(jax.random.randint(part_keys[7], (N_XY, N_GZ, SRC_DEV), 0, BINS), jax.random.fold_in(part_keys[7], 1), 0, BINS - 1).astype(jnp.int32)
    bin_weight = jnp.clip(jnp.exp(jax.random.uniform(part_keys[8], (BINS,), jnp.float32, math.log(0.5), math.log(2.0))), 0.5, 2.0)
    return {"fields": fields, "adjoint_fields": adjoint_fields, "material_ids": material_ids, "material_eps": material_eps, "monitor_cells": monitor_cells, "monitor_bins": monitor_bins, "source_cells": source_cells, "source_bins": source_bins, "bin_weight": bin_weight}


STEP_RATIO = 0.5

def forward_diff(values, after, along):
    upper = jnp.concatenate([lax.slice_in_dim(values, 1, values.shape[along], axis=along), jnp.expand_dims(after, along)], axis=along)
    return upper - values

def backward_diff(values, before, along):
    lower = jnp.concatenate([jnp.expand_dims(before, along), lax.slice_in_dim(values, 0, values.shape[along] - 1, axis=along)], axis=along)
    return values - lower

def update_magnetic(electric, magnetic):
    electric_x, electric_y, electric_z = electric
    magnetic_x, magnetic_y, magnetic_z = magnetic
    zero_x = jnp.zeros_like(electric_x[0])
    zero_z = jnp.zeros_like(electric_x[:, 0])
    zero_y = jnp.zeros_like(electric_x[:, :, 0])
    magnetic_x = magnetic_x - STEP_RATIO * (forward_diff(electric_z, zero_y, 2) - forward_diff(electric_y, zero_z, 1))
    magnetic_y = magnetic_y - STEP_RATIO * (forward_diff(electric_x, zero_z, 1) - forward_diff(electric_z, zero_x, 0))
    magnetic_z = magnetic_z - STEP_RATIO * (forward_diff(electric_y, zero_x, 0) - forward_diff(electric_x, zero_y, 2))
    return (magnetic_x, magnetic_y, magnetic_z)

def update_electric(electric, magnetic, inverse):
    electric_x, electric_y, electric_z = electric
    magnetic_x, magnetic_y, magnetic_z = magnetic
    zero_x = jnp.zeros_like(electric_x[0])
    zero_z = jnp.zeros_like(electric_x[:, 0])
    zero_y = jnp.zeros_like(electric_x[:, :, 0])
    electric_x = electric_x + STEP_RATIO * inverse * (backward_diff(magnetic_z, zero_y, 2) - backward_diff(magnetic_y, zero_z, 1))
    electric_y = electric_y + STEP_RATIO * inverse * (backward_diff(magnetic_x, zero_z, 1) - backward_diff(magnetic_z, zero_x, 0))
    electric_z = electric_z + STEP_RATIO * inverse * (backward_diff(magnetic_y, zero_x, 0) - backward_diff(magnetic_x, zero_y, 2))
    return (electric_x, electric_y, electric_z)

def inverse_permittivity(material_ids, material_eps):
    result = jnp.zeros(material_ids.shape, jnp.float32)
    for material in range(material_eps.shape[0]):
        result = jnp.where(material_ids == material, 1.0 / material_eps[material], result)
    return result

def time_kernels(count):
    times = jnp.arange(count, dtype=jnp.float32) + 1.0
    omegas = 0.3 + 0.35 * jnp.arange(NFREQ, dtype=jnp.float32)
    phases = times[:, None] * omegas[None, :]
    record_kernel = jnp.concatenate([jnp.cos(phases), -jnp.sin(phases)], axis=1)
    reverse = count - jnp.arange(count, dtype=jnp.float32)
    back_phases = reverse[:, None] * omegas[None, :]
    source_kernel = jnp.concatenate([jnp.cos(back_phases), jnp.sin(back_phases)], axis=1)
    return (record_kernel, source_kernel)

def normalize(totals, weights):
    real_part = totals[:NFREQ]
    imag_part = totals[NFREQ:]
    scale = weights[None, :] / jnp.sqrt(1.0 + real_part * real_part + imag_part * imag_part)
    return jnp.concatenate([real_part * scale, imag_part * scale], axis=0)

def global_cells(local_cells):
    tile_x = jnp.arange(N_XY, dtype=jnp.int32)[:, None, None]
    tile_z = jnp.arange(N_GZ, dtype=jnp.int32)[None, :, None]
    local_x = local_cells // (CZ * NY)
    local_z = local_cells // NY % CZ
    local_y = local_cells % NY
    return (((tile_x * CX + local_x) * NZ + tile_z * CZ + local_z) * NY + local_y).reshape(-1).astype(jnp.int32)

def reference(fields, adjoint_fields, material_ids, material_eps, monitor_cells, monitor_bins, source_cells, source_bins, bin_weight):
    inverse = inverse_permittivity(material_ids, material_eps)
    record_kernel, source_kernel = time_kernels(STEPS)
    watched = global_cells(monitor_cells)
    electric = (fields[0], fields[1], fields[2])
    magnetic = (fields[3], fields[4], fields[5])
    records = []
    for step_index in range(STEPS):
        magnetic = update_magnetic(electric, magnetic)
        electric = update_electric(electric, magnetic, inverse)
        records.append(electric[2].reshape(-1)[watched])
    forward_out = jnp.stack(list(electric) + list(magnetic))
    samples = jnp.stack(records)
    partial_dft = jnp.dot(samples.T, record_kernel, precision=lax.Precision.HIGHEST)
    monitor_dft = jax.ops.segment_sum(partial_dft, monitor_bins.reshape(-1), num_segments=BINS).T
    coefficients = normalize(monitor_dft, bin_weight)
    picked = jnp.take(coefficients, source_bins.reshape(-1), axis=1)
    amplitudes = jnp.dot(source_kernel, picked, precision=lax.Precision.HIGHEST)
    targets = global_cells(source_cells)
    electric = (adjoint_fields[0], adjoint_fields[1], adjoint_fields[2])
    magnetic = (adjoint_fields[3], adjoint_fields[4], adjoint_fields[5])
    for step_index in range(STEPS):
        magnetic = update_magnetic(electric, magnetic)
        electric = update_electric(electric, magnetic, inverse)
        driven = electric[2].reshape(-1).at[targets].add(amplitudes[step_index]).reshape(electric[2].shape)
        electric = (electric[0], electric[1], driven)
    adjoint_out = jnp.stack(list(electric) + list(magnetic))
    return (forward_out, adjoint_out, monitor_dft)
```

```python
import functools

import jax
import jax.numpy as jnp
import numpy as np
from jax import lax
from jax.experimental import pallas as pl
from jax.experimental.pallas import tpu as pltpu
from jax.sharding import PartitionSpec as P

STEPS = 8
NFREQ = 4
STEP_RATIO = 0.5


def from_behind(value, axis, steps):
    count = lax.axis_size(axis)
    first, last = (max(0, -steps), min(count, count - steps))
    return lax.ppermute(value, axis, [(source, source + steps) for source in range(first, last)])


def forward_diff(values, after, along):
    upper = jnp.concatenate(
        [
            lax.slice_in_dim(values, 1, values.shape[along], axis=along),
            jnp.expand_dims(after, along),
        ],
        axis=along,
    )
    return upper - values


def backward_diff(values, before, along):
    lower = jnp.concatenate(
        [
            jnp.expand_dims(before, along),
            lax.slice_in_dim(values, 0, values.shape[along] - 1, axis=along),
        ],
        axis=along,
    )
    return values - lower


def update_magnetic(electric, magnetic):
    electric_x, electric_y, electric_z = electric
    magnetic_x, magnetic_y, magnetic_z = magnetic
    x_next = from_behind(jnp.stack([electric_y[0], electric_z[0]]), "xy", -1)
    z_next = from_behind(jnp.stack([electric_x[:, 0], electric_y[:, 0]]), "gz", -1)
    zero_y = jnp.zeros_like(electric_x[:, :, 0])
    magnetic_x = magnetic_x - STEP_RATIO * (
        forward_diff(electric_z, zero_y, 2) - forward_diff(electric_y, z_next[1], 1)
    )
    magnetic_y = magnetic_y - STEP_RATIO * (
        forward_diff(electric_x, z_next[0], 1) - forward_diff(electric_z, x_next[1], 0)
    )
    magnetic_z = magnetic_z - STEP_RATIO * (
        forward_diff(electric_y, x_next[0], 0) - forward_diff(electric_x, zero_y, 2)
    )
    return (magnetic_x, magnetic_y, magnetic_z)


def update_electric(electric, magnetic, inverse):
    electric_x, electric_y, electric_z = electric
    magnetic_x, magnetic_y, magnetic_z = magnetic
    x_prev = from_behind(jnp.stack([magnetic_y[-1], magnetic_z[-1]]), "xy", 1)
    z_prev = from_behind(jnp.stack([magnetic_x[:, -1], magnetic_y[:, -1]]), "gz", 1)
    zero_y = jnp.zeros_like(electric_x[:, :, 0])
    electric_x = electric_x + STEP_RATIO * inverse * (
        backward_diff(magnetic_z, zero_y, 2) - backward_diff(magnetic_y, z_prev[1], 1)
    )
    electric_y = electric_y + STEP_RATIO * inverse * (
        backward_diff(magnetic_x, z_prev[0], 1) - backward_diff(magnetic_z, x_prev[1], 0)
    )
    electric_z = electric_z + STEP_RATIO * inverse * (
        backward_diff(magnetic_y, x_prev[0], 0) - backward_diff(magnetic_x, zero_y, 2)
    )
    return (electric_x, electric_y, electric_z)


def inverse_permittivity(material_ids, material_eps):
    result = jnp.zeros(material_ids.shape, jnp.float32)
    for material in range(material_eps.shape[0]):
        result = jnp.where(material_ids == material, 1.0 / material_eps[material], result)
    return result


def time_kernels(count):
    times = np.arange(count) + 1.0
    omegas = 0.3 + 0.35 * np.arange(NFREQ)
    phases = times[:, None] * omegas[None, :]
    record_kernel = np.concatenate([np.cos(phases), -np.sin(phases)], axis=1)
    reverse = count - np.arange(count)
    back_phases = reverse[:, None] * omegas[None, :]
    source_kernel = np.concatenate([np.cos(back_phases), np.sin(back_phases)], axis=1)
    return (record_kernel.astype(np.float32), source_kernel.astype(np.float32))


def normalize(totals, weights):
    real_part = totals[:NFREQ]
    imag_part = totals[NFREQ:]
    scale = weights / jnp.sqrt(1.0 + real_part * real_part + imag_part * imag_part)
    return jnp.concatenate([real_part * scale, imag_part * scale], axis=0)


def local_general(
    fields,
    adjoint_fields,
    material_ids,
    material_eps,
    monitor_cells,
    monitor_bins,
    source_cells,
    source_bins,
    bin_weight,
):
    inverse = inverse_permittivity(material_ids, material_eps)
    record_kernel, source_kernel = time_kernels(STEPS)
    watched = monitor_cells.reshape(-1)
    electric = (fields[0], fields[1], fields[2])
    magnetic = (fields[3], fields[4], fields[5])
    records = []
    for _ in range(STEPS):
        magnetic = update_magnetic(electric, magnetic)
        electric = update_electric(electric, magnetic, inverse)
        records.append(electric[2].reshape(-1)[watched])
    forward_out = jnp.stack(list(electric) + list(magnetic))
    samples = jnp.stack(records)
    partial_dft = jnp.dot(samples.T, record_kernel, precision=lax.Precision.HIGHEST)
    bin_table = jax.ops.segment_sum(
        partial_dft, monitor_bins.reshape(-1), num_segments=bin_weight.shape[0]
    ).T
    owners = lax.axis_size("xy") * lax.axis_size("gz")
    own_count = bin_table.shape[1] // owners
    device_rank = lax.axis_index(("xy", "gz"))
    totals = lax.psum(bin_table, ("xy", "gz"))
    monitor_dft = lax.dynamic_slice_in_dim(totals, device_rank * own_count, own_count, axis=1)
    coefficients = normalize(totals, bin_weight[None, :])
    picked = jnp.take(coefficients, source_bins.reshape(-1), axis=1)
    amplitudes = jnp.dot(source_kernel, picked, precision=lax.Precision.HIGHEST)
    targets = source_cells.reshape(-1)
    electric = (adjoint_fields[0], adjoint_fields[1], adjoint_fields[2])
    magnetic = (adjoint_fields[3], adjoint_fields[4], adjoint_fields[5])
    for step_index in range(STEPS):
        magnetic = update_magnetic(electric, magnetic)
        electric = update_electric(electric, magnetic, inverse)
        driven = (
            electric[2]
            .reshape(-1)
            .at[targets]
            .add(amplitudes[step_index])
            .reshape(electric[2].shape)
        )
        electric = (electric[0], electric[1], driven)
    adjoint_out = jnp.stack(list(electric) + list(magnetic))
    return (forward_out, adjoint_out, monitor_dft)


TILES = 4
CX = 4
CZ = 16
LANES = 128
HALO = 8
ROWS = CZ + 2 * HALO
WIDE = 2 * LANES
PLANES = TILES * CX
ENTRIES = 1024
SUB = 8
ZT = CZ // SUB
BF16 = jnp.bfloat16
F32 = jnp.float32


def packed_rows(parts):
    return parts * CX + (parts + 1) // 2


def lane_ids():
    return lax.broadcasted_iota(jnp.int32, (SUB, LANES), 1)


def pack_block(read, parts, column, store):
    lanes = lane_ids()
    upper = lanes >= LANES // 2
    take_left = jnp.logical_and(upper, column > 0)
    take_right = jnp.logical_and(jnp.logical_not(upper), column < TILES - 1)
    here = pl.multiple_of(column * LANES, LANES)
    left = pl.multiple_of(jnp.maximum(column - 1, 0) * LANES, LANES)
    right = pl.multiple_of(jnp.minimum(column + 1, TILES - 1) * LANES, LANES)
    size = packed_rows(parts)
    for zt in range(ZT):
        margins = [jnp.zeros((SUB, LANES), F32) for _ in range((parts + 1) // 2)]
        for part in range(parts):
            for x in range(CX):
                store(zt * size + part * CX + x, read(part, x, zt, here))
                both = jnp.where(
                    take_left,
                    read(part, x, zt, left),
                    jnp.where(take_right, read(part, x, zt, right), 0.0),
                )
                slot = (part % 2) * CX + x
                placed = pltpu.roll(both, (16 * slot + HALO) % LANES, 1)
                margins[part // 2] = jnp.where(lanes // 16 == slot, placed, margins[part // 2])
        for pair, margin in enumerate(margins):
            store(zt * size + parts * CX + pair, margin)


def pack_forward_kernel(
    fields_ref, ids_ref, eps_ref, cells_ref, bins_ref, o0, o1, o2, o3, inverse_ref
):
    me = lax.axis_index("xy")
    ids = ids_ref[...]
    eps = jnp.full(ids.shape, eps_ref[0], F32)
    for material in range(1, eps_ref.shape[0]):
        eps = jnp.where(ids == material, eps_ref[material], eps)
    inverse_ref[...] = STEP_RATIO * (1.0 / eps)

    def read(part, x, zt, lane):
        rows = pl.ds(zt * SUB, SUB)
        if part == 6:
            return inverse_ref[x, rows, pl.ds(lane, LANES)]
        return fields_ref[part, x, rows, pl.ds(lane, LANES)]

    for m, out in enumerate((o0, o1, o2, o3)):

        def store(row, value, out=out):
            out[row] = value

        pack_block(read, 7, me ^ m, store)
        out[ZT * packed_rows(7)] = cells_ref[...].astype(F32)
        out[ZT * packed_rows(7) + 1] = bins_ref[...].astype(F32)


def pack_adjoint_kernel(fields_ref, cells_ref, bins_ref, o0, o1, o2, o3):
    me = lax.axis_index("xy")

    def read(part, x, zt, lane):
        return fields_ref[part, x, pl.ds(zt * SUB, SUB), pl.ds(lane, LANES)]

    for m, out in enumerate((o0, o1, o2, o3)):

        def store(row, value, out=out):
            out[row] = value

        pack_block(read, 6, me ^ m, store)
        out[ZT * packed_rows(6)] = cells_ref[...].astype(F32) + 1.0
        out[ZT * packed_rows(6) + 1] = bins_ref[...].astype(F32)


def slab_kernel(size, lists, b0, b1, b2, b3, first_ref, second_ref):
    even = lax.rem(lax.axis_index("gz"), 2) == 0
    zt_first = jnp.where(even, 1, 0)
    for m, block in enumerate((b0, b1, b2, b3)):
        base = m * (size + lists)
        first_ref[pl.ds(base, size)] = block[pl.ds(zt_first * size, size)]
        second_ref[pl.ds(base, size)] = block[pl.ds((1 - zt_first) * size, size)]
        for k in range(lists):
            first_ref[base + size + k] = block[ZT * size + k]
            second_ref[base + size + k] = block[ZT * size + k]


def unpack(parts, lists, blocks, first_ref, second_ref, put):
    me = lax.axis_index("xy")
    even = lax.rem(lax.axis_index("gz"), 2) == 0
    row_first = pl.multiple_of(jnp.where(even, HALO + CZ, 0), SUB)
    row_second = pl.multiple_of(jnp.where(even, 0, HALO + CZ), SUB)
    size = packed_rows(parts)
    lanes = lane_ids()
    in_margin = jnp.logical_or(lanes < HALO, lanes >= LANES - HALO)
    for m, block in enumerate(blocks):
        base = (me ^ m) * CX + 1
        sources = (
            (first_ref, m * (size + lists), row_first),
            (second_ref, m * (size + lists), row_second),
            (block, 0, HALO),
            (block, size, HALO + SUB),
        )
        for ref, start, row in sources:
            for part in range(parts):
                for x in range(CX):
                    slot = (part % 2) * CX + x
                    margin = pltpu.roll(
                        ref[start + parts * CX + part // 2], (-16 * slot - HALO) % LANES, 1
                    )
                    put(
                        part,
                        base + x,
                        row,
                        ref[start + part * CX + x],
                        jnp.where(in_margin, margin, 0.0),
                    )


def magnetic_factor():
    rows = lax.broadcasted_iota(jnp.int32, (ROWS, WIDE), 0)
    lanes = lax.broadcasted_iota(jnp.int32, (ROWS, WIDE), 1)
    below_z = jnp.logical_and(rows < HALO, lax.axis_index("gz") == 0)
    below_y = jnp.logical_and(lanes >= WIDE - 2 * HALO, lax.axis_index("xy") == 0)
    return jnp.where(jnp.logical_or(below_z, below_y), 0.0, STEP_RATIO)


def step_plane(f, factor_ref, inverse_ref, i):
    def z_up(v):
        return pltpu.roll(v, ROWS - 1, 0)

    def z_down(v):
        return pltpu.roll(v, 1, 0)

    def y_up(v):
        return pltpu.roll(v, WIDE - 1, 1)

    def y_down(v):
        return pltpu.roll(v, 1, 1)

    factor = factor_ref[...]
    ex, ey, ez = f[0, i], f[1, i], f[2, i]
    hx = f[3, i] - factor * ((y_up(ez) - ez) - (z_up(ey) - ey))
    hy = f[4, i] - factor * ((z_up(ex) - ex) - (f[2, i + 1] - ez))
    hz = f[5, i] - factor * ((f[1, i + 1] - ey) - (y_up(ex) - ex))
    f[3, i] = hx
    f[4, i] = hy
    f[5, i] = hz
    inverse = inverse_ref[i]
    ex = ex + inverse * ((hz - y_down(hz)) - (hy - z_down(hy)))
    ey = ey + inverse * ((hx - z_down(hx)) - (hz - f[5, i - 1]))
    ez = ez + inverse * ((hy - f[4, i - 1]) - (hx - y_down(hx)))
    f[0, i] = ex
    f[1, i] = ey
    return ez


def entry_row(vector):
    whole = vector.astype(jnp.int32)
    return jnp.concatenate([whole[i : i + 1] for i in range(SUB)], axis=1)


def one_hot(rows, index):
    ids = lax.broadcasted_iota(jnp.int32, (rows, index.shape[1]), 0)
    return jnp.where(ids == index, 1.0, 0.0).astype(BF16)


def split(values):
    high = values.astype(BF16)
    return high, (values - high.astype(F32)).astype(BF16)


def write_back(f, outs):
    me = lax.axis_index("xy")
    for m, out in enumerate(outs):
        base = (me ^ m) * CX + 1
        for part in range(6):
            for x in range(CX):
                for zt in range(ZT):
                    out[(part * CX + x) * ZT + zt] = f[
                        part, base + x, HALO + zt * SUB : HALO + (zt + 1) * SUB, 0:LANES
                    ]


def clear_edges(f):
    for part in range(6):
        f[part, 0] = jnp.zeros((ROWS, WIDE), F32)
        f[part, PLANES + 1] = jnp.zeros((ROWS, WIDE), F32)


def forward_kernel(
    b0, b1, b2, b3, first_ref, second_ref, kernel_ref,
    o0, o1, o2, o3, inverse_ref, table_ref,
    f, factor_ref, high_ref, low_ref, sums_ref,
):
    me = lax.axis_index("xy")
    blocks = (b0, b1, b2, b3)
    clear_edges(f)

    def put(part, plane, row, columns, margins):
        if part == 6:
            inverse_ref[plane, pl.ds(row, SUB), 0:LANES] = columns
            inverse_ref[plane, pl.ds(row, SUB), LANES:WIDE] = margins
        else:
            f[part, plane, pl.ds(row, SUB), 0:LANES] = columns
            f[part, plane, pl.ds(row, SUB), LANES:WIDE] = margins

    unpack(7, 0, blocks, first_ref, second_ref, put)
    factor_ref[...] = magnetic_factor()

    def step(t, carry):
        def plane(i, carry):
            ez = step_plane(f, factor_ref, inverse_ref, i)
            f[2, i] = ez
            high, low = split(ez[HALO : HALO + CZ, 0:LANES])
            high_ref[(i - 1) // CX, t, lax.rem(i - 1, CX)] = high
            low_ref[(i - 1) // CX, t, lax.rem(i - 1, CX)] = low
            return carry

        return lax.fori_loop(1, PLANES + 1, plane, carry)

    lax.fori_loop(0, STEPS, step, 0)
    write_back(f, (o0, o1, o2, o3))

    bins = table_ref.shape[1]
    per_tile = CX * CZ
    rows = STEPS * per_tile
    sums_ref[...] = jnp.zeros_like(sums_ref)
    lists = ZT * packed_rows(7)
    for m, block in enumerate(blocks):
        cells = entry_row(block[lists])
        where = jnp.where((cells // LANES) % TILES == me, cells // (LANES * TILES), -1)
        lane_hot = one_hot(LANES, cells % LANES)
        bin_hot = one_hot(bins, entry_row(block[lists + 1]))
        row_ids = lax.broadcasted_iota(jnp.int32, (per_tile, ENTRIES), 0)
        hit = row_ids == where
        for ref in (high_ref, low_ref):
            for t in range(STEPS):
                values = ref[me ^ m, t].reshape(per_tile, LANES)
                at_lane = jnp.dot(values, lane_hot, preferred_element_type=F32)
                picked = jnp.where(hit, at_lane, 0.0).astype(BF16)
                sums_ref[t * per_tile : (t + 1) * per_tile] += lax.dot_general(
                    picked, bin_hot, (((1,), (1,)), ((), ())), preferred_element_type=F32
                )
    table_ref[...] = jnp.dot(
        kernel_ref[...],
        sums_ref[...],
        precision=lax.Precision.HIGHEST,
        preferred_element_type=F32,
    )


def adjoint_kernel(
    b0, b1, b2, b3, first_ref, second_ref, inverse_ref, totals_ref, weight_ref, kernel_ref,
    o0, o1, o2, o3,
    f, factor_ref, drive_ref,
):
    me = lax.axis_index("xy")
    even = lax.rem(lax.axis_index("gz"), 2) == 0
    blocks = (b0, b1, b2, b3)
    clear_edges(f)

    def put(part, plane, row, columns, margins):
        f[part, plane, pl.ds(row, SUB), 0:LANES] = columns
        f[part, plane, pl.ds(row, SUB), LANES:WIDE] = margins

    unpack(6, 2, blocks, first_ref, second_ref, put)
    factor_ref[...] = magnetic_factor()

    totals = totals_ref[...]
    bins = totals.shape[1]
    coefficients = normalize(totals, weight_ref[...])
    by_bin = jnp.zeros((STEPS, bins), F32)
    for k in range(2 * NFREQ):
        by_bin = by_bin + kernel_ref[:, k : k + 1] * coefficients[k : k + 1, :]
    bin_high, bin_low = split(by_bin)

    def drive(ref, start, planes, z_first, z_count, row):
        cells = entry_row(ref[start]) - 1
        bin_hot = one_hot(bins, entry_row(ref[start + 1]))
        columns = cells % (LANES * TILES) - me * LANES
        inside = jnp.logical_and(columns >= -HALO, columns < LANES + HALO)
        inside = jnp.logical_and(inside, cells >= 0)
        lane_hot = one_hot(WIDE, jnp.where(inside, columns % WIDE, -1))
        z = (cells // (LANES * TILES)) % CZ - z_first
        x = cells // (LANES * TILES * CZ)
        kept = jnp.logical_and(z >= 0, z < z_count)
        where = jnp.where(kept, x * z_count + z, -1)
        hit = lax.broadcasted_iota(jnp.int32, (CX * z_count, ENTRIES), 0) == where
        amplitude = [
            jnp.dot(part, bin_hot, preferred_element_type=F32) for part in (bin_high, bin_low)
        ]
        for t in range(STEPS):
            total = jnp.zeros((CX * z_count, WIDE), F32)
            for part in amplitude:
                spread = jnp.where(hit, part[t : t + 1, :], 0.0).astype(BF16)
                total = total + lax.dot_general(
                    spread, lane_hot, (((1,), (1,)), ((), ())), preferred_element_type=F32
                )
            for k in range(CX):
                drive_ref[t, planes + k, pl.ds(row, z_count), :] = total[
                    k * z_count : (k + 1) * z_count
                ]

    size = packed_rows(6)
    z_first = jnp.where(even, 0, HALO)
    row_first = pl.multiple_of(jnp.where(even, HALO + CZ, 0), SUB)
    row_second = pl.multiple_of(jnp.where(even, 0, HALO + CZ), SUB)
    for m, block in enumerate(blocks):
        planes = (me ^ m) * CX
        drive(block, ZT * size, planes, 0, CZ, HALO)
        drive(first_ref, m * (size + 2) + size, planes, z_first, HALO, row_first)
        drive(second_ref, m * (size + 2) + size, planes, HALO - z_first, HALO, row_second)

    def step(t, carry):
        def plane(i, carry):
            ez = step_plane(f, factor_ref, inverse_ref, i)
            f[2, i] = ez + drive_ref[t, i - 1]
            return carry

        return lax.fori_loop(1, PLANES + 1, plane, carry)

    lax.fori_loop(0, STEPS, step, 0)
    write_back(f, (o0, o1, o2, o3))


def spread_kernel(b0, b1, b2, b3, out_ref):
    me = lax.axis_index("xy")
    for m, block in enumerate((b0, b1, b2, b3)):
        lane = pl.multiple_of((me ^ m) * LANES, LANES)
        for part in range(6):
            for x in range(CX):
                for zt in range(ZT):
                    out_ref[part, x, zt * SUB : (zt + 1) * SUB, pl.ds(lane, LANES)] = block[
                        (part * CX + x) * ZT + zt
                    ]


def struct(*shape):
    return jax.ShapeDtypeStruct(shape, F32)


def in_vmem(count):
    return [pl.BlockSpec(memory_space=pltpu.VMEM)] * count


def call(kernel, args, outs, scratch=(), scalars=()):
    specs = in_vmem(len(args))
    for place in scalars:
        specs[place] = pl.BlockSpec(memory_space=pltpu.SMEM)
    single = not isinstance(outs, list)
    return pl.pallas_call(
        kernel,
        out_shape=outs,
        in_specs=specs,
        out_specs=pl.BlockSpec(memory_space=pltpu.VMEM) if single else in_vmem(len(outs)),
        scratch_shapes=list(scratch),
        compiler_params=pltpu.CompilerParams(vmem_limit_bytes=48 * 1024 * 1024),
    )(*args)


def swap(value, axis, distance):
    count = lax.axis_size(axis)
    return lax.ppermute(value, axis, [(i, i ^ distance) for i in range(count)])


def swap_blocks(blocks):
    return [blocks[0]] + [swap(blocks[m], "xy", m) for m in range(1, TILES)]


def swap_neighbours(first, second):
    count = lax.axis_size("gz")
    pairs = [(i, i ^ 1) for i in range(count) if i ^ 1 < count]
    others = [(i, ((i + 1) ^ 1) - 1) for i in range(count)]
    others = [(i, j) for i, j in others if 0 <= j < count]
    return lax.ppermute(first, "gz", pairs), lax.ppermute(second, "gz", others)


def sum_all(table):
    for axis in ("xy", "gz"):
        distance = 1
        while distance < lax.axis_size(axis):
            table = table + swap(table, axis, distance)
            distance *= 2
    return table


def local_columns(
    fields,
    adjoint_fields,
    material_ids,
    material_eps,
    monitor_cells,
    monitor_bins,
    source_cells,
    source_bins,
    bin_weight,
):
    bins = bin_weight.shape[0]
    record_kernel, source_kernel = time_kernels(STEPS)
    by_row = np.repeat(record_kernel.T, CX * CZ, axis=1)
    lists = [
        v.reshape(SUB, LANES) for v in (monitor_cells, monitor_bins, source_cells, source_bins)
    ]
    n_fwd, n_adj = packed_rows(7), packed_rows(6)
    sent = call(
        pack_forward_kernel,
        (fields, material_ids, material_eps, lists[0], lists[1]),
        [struct(ZT * n_fwd + 2, SUB, LANES)] * TILES,
        [pltpu.VMEM((CX, CZ, TILES * LANES), F32)],
        scalars=(2,),
    )
    adjoint_sent = call(
        pack_adjoint_kernel,
        (adjoint_fields, lists[2], lists[3]),
        [struct(ZT * n_adj + 2, SUB, LANES)] * TILES,
    )
    blocks = swap_blocks(sent)
    slabs = call(
        functools.partial(slab_kernel, n_fwd, 0), blocks, [struct(TILES * n_fwd, SUB, LANES)] * 2
    )
    slabs, adjoint_sent = lax.optimization_barrier((slabs, adjoint_sent))
    first, second = swap_neighbours(*slabs)
    adjoint_blocks = swap_blocks(adjoint_sent)
    (first, second), adjoint_blocks = lax.optimization_barrier(((first, second), adjoint_blocks))
    adjoint_slabs = call(
        functools.partial(slab_kernel, n_adj, 2),
        adjoint_blocks,
        [struct(TILES * (n_adj + 2), SUB, LANES)] * 2,
    )
    adjoint_first, adjoint_second = swap_neighbours(*adjoint_slabs)
    field = pltpu.VMEM((6, PLANES + 2, ROWS, WIDE), F32)
    factor = pltpu.VMEM((ROWS, WIDE), F32)
    record = pltpu.VMEM((TILES, STEPS, CX, CZ, LANES), BF16)
    *forward_sent, inverse, table = call(
        forward_kernel,
        (*blocks, first, second, by_row),
        [struct(6 * CX * ZT, SUB, LANES)] * TILES
        + [struct(PLANES + 2, ROWS, WIDE), struct(2 * NFREQ, bins)],
        [field, factor, record, record, pltpu.VMEM((STEPS * CX * CZ, bins), F32)],
    )
    totals = sum_all(table)
    forward_blocks = swap_blocks(forward_sent)
    own_count = bins // (lax.axis_size("xy") * lax.axis_size("gz"))
    device_rank = lax.axis_index(("xy", "gz"))
    monitor_dft = lax.dynamic_slice_in_dim(totals, device_rank * own_count, own_count, axis=1)
    adjoint_back = call(
        adjoint_kernel,
        (
            *adjoint_blocks,
            adjoint_first,
            adjoint_second,
            inverse,
            totals,
            bin_weight.reshape(1, bins),
            source_kernel,
        ),
        [struct(6 * CX * ZT, SUB, LANES)] * TILES,
        [field, factor, pltpu.VMEM((STEPS, PLANES, ROWS, WIDE), F32)],
    )
    forward_out = call(spread_kernel, forward_blocks, struct(*fields.shape))
    adjoint_out = call(spread_kernel, swap_blocks(adjoint_back), struct(*fields.shape))
    return (forward_out, adjoint_out, monitor_dft)


def solution(mesh):
    placed = (
        P("grp", "xy", "gz", None),
        P("grp", "xy", "gz", None),
        P("xy", "gz", "grp"),
        P(),
        P("xy", "gz", "grp"),
        P("xy", "gz", "grp"),
        P("xy", "gz", "grp"),
        P("xy", "gz", "grp"),
        P("grp"),
    )
    columns = mesh.shape["xy"] == TILES and mesh.shape["gz"] & (mesh.shape["gz"] - 1) == 0
    return jax.shard_map(
        local_columns if columns else local_general,
        mesh=mesh,
        in_specs=placed,
        out_specs=(P("grp", "xy", "gz", None), P("grp", "xy", "gz", None), P("grp", ("xy", "gz"))),
        check_vma=False,
    )
```

```python
import functools

import jax
import jax.numpy as jnp
import numpy as np
from jax import lax
from jax.experimental import pallas as pl
from jax.experimental.pallas import tpu as pltpu
from jax.sharding import PartitionSpec as P

STEPS = 8
NFREQ = 4
STEP_RATIO = 0.5


def from_behind(value, axis, steps):
    count = lax.axis_size(axis)
    first, last = (max(0, -steps), min(count, count - steps))
    return lax.ppermute(value, axis, [(source, source + steps) for source in range(first, last)])


def forward_diff(values, after, along):
    upper = jnp.concatenate(
        [
            lax.slice_in_dim(values, 1, values.shape[along], axis=along),
            jnp.expand_dims(after, along),
        ],
        axis=along,
    )
    return upper - values


def backward_diff(values, before, along):
    lower = jnp.concatenate(
        [
            jnp.expand_dims(before, along),
            lax.slice_in_dim(values, 0, values.shape[along] - 1, axis=along),
        ],
        axis=along,
    )
    return values - lower


def update_magnetic(electric, magnetic):
    electric_x, electric_y, electric_z = electric
    magnetic_x, magnetic_y, magnetic_z = magnetic
    x_next = from_behind(jnp.stack([electric_y[0], electric_z[0]]), "xy", -1)
    z_next = from_behind(jnp.stack([electric_x[:, 0], electric_y[:, 0]]), "gz", -1)
    zero_y = jnp.zeros_like(electric_x[:, :, 0])
    magnetic_x = magnetic_x - STEP_RATIO * (
        forward_diff(electric_z, zero_y, 2) - forward_diff(electric_y, z_next[1], 1)
    )
    magnetic_y = magnetic_y - STEP_RATIO * (
        forward_diff(electric_x, z_next[0], 1) - forward_diff(electric_z, x_next[1], 0)
    )
    magnetic_z = magnetic_z - STEP_RATIO * (
        forward_diff(electric_y, x_next[0], 0) - forward_diff(electric_x, zero_y, 2)
    )
    return (magnetic_x, magnetic_y, magnetic_z)


def update_electric(electric, magnetic, inverse):
    electric_x, electric_y, electric_z = electric
    magnetic_x, magnetic_y, magnetic_z = magnetic
    x_prev = from_behind(jnp.stack([magnetic_y[-1], magnetic_z[-1]]), "xy", 1)
    z_prev = from_behind(jnp.stack([magnetic_x[:, -1], magnetic_y[:, -1]]), "gz", 1)
    zero_y = jnp.zeros_like(electric_x[:, :, 0])
    electric_x = electric_x + STEP_RATIO * inverse * (
        backward_diff(magnetic_z, zero_y, 2) - backward_diff(magnetic_y, z_prev[1], 1)
    )
    electric_y = electric_y + STEP_RATIO * inverse * (
        backward_diff(magnetic_x, z_prev[0], 1) - backward_diff(magnetic_z, x_prev[1], 0)
    )
    electric_z = electric_z + STEP_RATIO * inverse * (
        backward_diff(magnetic_y, x_prev[0], 0) - backward_diff(magnetic_x, zero_y, 2)
    )
    return (electric_x, electric_y, electric_z)


def inverse_permittivity(material_ids, material_eps):
    result = jnp.zeros(material_ids.shape, jnp.float32)
    for material in range(material_eps.shape[0]):
        result = jnp.where(material_ids == material, 1.0 / material_eps[material], result)
    return result


def time_kernels(count):
    times = np.arange(count) + 1.0
    omegas = 0.3 + 0.35 * np.arange(NFREQ)
    phases = times[:, None] * omegas[None, :]
    record_kernel = np.concatenate([np.cos(phases), -np.sin(phases)], axis=1)
    reverse = count - np.arange(count)
    back_phases = reverse[:, None] * omegas[None, :]
    source_kernel = np.concatenate([np.cos(back_phases), np.sin(back_phases)], axis=1)
    return (record_kernel.astype(np.float32), source_kernel.astype(np.float32))


def normalize(totals, weights):
    real_part = totals[:NFREQ]
    imag_part = totals[NFREQ:]
    scale = weights / jnp.sqrt(1.0 + real_part * real_part + imag_part * imag_part)
    return jnp.concatenate([real_part * scale, imag_part * scale], axis=0)


def local_general(
    fields,
    adjoint_fields,
    material_ids,
    material_eps,
    monitor_cells,
    monitor_bins,
    source_cells,
    source_bins,
    bin_weight,
):
    inverse = inverse_permittivity(material_ids, material_eps)
    record_kernel, source_kernel = time_kernels(STEPS)
    watched = monitor_cells.reshape(-1)
    electric = (fields[0], fields[1], fields[2])
    magnetic = (fields[3], fields[4], fields[5])
    records = []
    for _ in range(STEPS):
        magnetic = update_magnetic(electric, magnetic)
        electric = update_electric(electric, magnetic, inverse)
        records.append(electric[2].reshape(-1)[watched])
    forward_out = jnp.stack(list(electric) + list(magnetic))
    samples = jnp.stack(records)
    partial_dft = jnp.dot(samples.T, record_kernel, precision=lax.Precision.HIGHEST)
    bin_table = jax.ops.segment_sum(
        partial_dft, monitor_bins.reshape(-1), num_segments=bin_weight.shape[0]
    ).T
    owners = lax.axis_size("xy") * lax.axis_size("gz")
    own_count = bin_table.shape[1] // owners
    device_rank = lax.axis_index(("xy", "gz"))
    totals = lax.psum(bin_table, ("xy", "gz"))
    monitor_dft = lax.dynamic_slice_in_dim(totals, device_rank * own_count, own_count, axis=1)
    coefficients = normalize(totals, bin_weight[None, :])
    picked = jnp.take(coefficients, source_bins.reshape(-1), axis=1)
    amplitudes = jnp.dot(source_kernel, picked, precision=lax.Precision.HIGHEST)
    targets = source_cells.reshape(-1)
    electric = (adjoint_fields[0], adjoint_fields[1], adjoint_fields[2])
    magnetic = (adjoint_fields[3], adjoint_fields[4], adjoint_fields[5])
    for step_index in range(STEPS):
        magnetic = update_magnetic(electric, magnetic)
        electric = update_electric(electric, magnetic, inverse)
        driven = (
            electric[2]
            .reshape(-1)
            .at[targets]
            .add(amplitudes[step_index])
            .reshape(electric[2].shape)
        )
        electric = (electric[0], electric[1], driven)
    adjoint_out = jnp.stack(list(electric) + list(magnetic))
    return (forward_out, adjoint_out, monitor_dft)


TILES = 4
CX = 4
CZ = 16
LANES = 128
HALO = 8
ROWS = CZ + 2 * HALO
PAD = 8
GROUP = 2
WIDE = 2 * LANES
PLANES = TILES * CX
ENTRIES = 1024
CHUNK = 256
SUB = 8
ZT = CZ // SUB
BF16 = jnp.bfloat16
F32 = jnp.float32


def packed_rows(parts):
    return parts * CX + (parts + 1) // 2


def lane_ids():
    return lax.broadcasted_iota(jnp.int32, (SUB, LANES), 1)


def pack_block(read, parts, column, store):
    lanes = lane_ids()
    upper = lanes >= LANES // 2
    take_left = jnp.logical_and(upper, column > 0)
    take_right = jnp.logical_and(jnp.logical_not(upper), column < TILES - 1)
    here = pl.multiple_of(column * LANES, LANES)
    left = pl.multiple_of(jnp.maximum(column - 1, 0) * LANES, LANES)
    right = pl.multiple_of(jnp.minimum(column + 1, TILES - 1) * LANES, LANES)
    size = packed_rows(parts)
    for zt in range(ZT):
        margins = [jnp.zeros((SUB, LANES), F32) for _ in range((parts + 1) // 2)]
        for part in range(parts):
            for x in range(CX):
                store(zt * size + part * CX + x, read(part, x, zt, here))
                both = jnp.where(
                    take_left,
                    read(part, x, zt, left),
                    jnp.where(take_right, read(part, x, zt, right), 0.0),
                )
                slot = (part % 2) * CX + x
                placed = pltpu.roll(both, (16 * slot + HALO) % LANES, 1)
                margins[part // 2] = jnp.where(lanes // 16 == slot, placed, margins[part // 2])
        for pair, margin in enumerate(margins):
            store(zt * size + parts * CX + pair, margin)


def pack_forward_kernel(
    fields_ref, ids_ref, eps_ref, cells_ref, bins_ref, o0, o1, o2, o3, inverse_ref
):
    me = lax.axis_index("xy")
    ids = ids_ref[...]
    eps = jnp.full(ids.shape, eps_ref[0], F32)
    for material in range(1, eps_ref.shape[0]):
        eps = jnp.where(ids == material, eps_ref[material], eps)
    inverse_ref[...] = STEP_RATIO * (1.0 / eps)

    def read(part, x, zt, lane):
        rows = pl.ds(zt * SUB, SUB)
        if part == 6:
            return inverse_ref[x, rows, pl.ds(lane, LANES)]
        return fields_ref[part, x, rows, pl.ds(lane, LANES)]

    for m, out in enumerate((o0, o1, o2, o3)):

        def store(row, value, out=out):
            out[row] = value

        pack_block(read, 7, me ^ m, store)
        out[ZT * packed_rows(7)] = cells_ref[...].astype(F32)
        out[ZT * packed_rows(7) + 1] = bins_ref[...].astype(F32)


def pack_adjoint_kernel(fields_ref, cells_ref, bins_ref, o0, o1, o2, o3):
    me = lax.axis_index("xy")

    def read(part, x, zt, lane):
        return fields_ref[part, x, pl.ds(zt * SUB, SUB), pl.ds(lane, LANES)]

    for m, out in enumerate((o0, o1, o2, o3)):

        def store(row, value, out=out):
            out[row] = value

        pack_block(read, 6, me ^ m, store)
        out[ZT * packed_rows(6)] = cells_ref[...].astype(F32) + 1.0
        out[ZT * packed_rows(6) + 1] = bins_ref[...].astype(F32)


def slab_kernel(size, lists, b0, b1, b2, b3, first_ref, second_ref):
    even = lax.rem(lax.axis_index("gz"), 2) == 0
    zt_first = jnp.where(even, 1, 0)
    for m, block in enumerate((b0, b1, b2, b3)):
        base = m * (size + lists)
        first_ref[pl.ds(base, size)] = block[pl.ds(zt_first * size, size)]
        second_ref[pl.ds(base, size)] = block[pl.ds((1 - zt_first) * size, size)]
        for k in range(lists):
            first_ref[base + size + k] = block[ZT * size + k]
            second_ref[base + size + k] = block[ZT * size + k]


def unpack(parts, lists, blocks, first_ref, second_ref, put):
    me = lax.axis_index("xy")
    even = lax.rem(lax.axis_index("gz"), 2) == 0
    row_first = pl.multiple_of(jnp.where(even, HALO + CZ, 0), SUB)
    row_second = pl.multiple_of(jnp.where(even, 0, HALO + CZ), SUB)
    size = packed_rows(parts)
    lanes = lane_ids()
    in_margin = jnp.logical_or(lanes < HALO, lanes >= LANES - HALO)
    for m, block in enumerate(blocks):
        base = (me ^ m) * CX + 1
        sources = (
            (first_ref, m * (size + lists), row_first),
            (second_ref, m * (size + lists), row_second),
            (block, 0, HALO),
            (block, size, HALO + SUB),
        )
        for ref, start, row in sources:
            for part in range(parts):
                for x in range(CX):
                    slot = (part % 2) * CX + x
                    margin = pltpu.roll(
                        ref[start + parts * CX + part // 2], (-16 * slot - HALO) % LANES, 1
                    )
                    put(
                        part,
                        base + x,
                        row,
                        ref[start + part * CX + x],
                        jnp.where(in_margin, margin, 0.0),
                    )


def magnetic_factor():
    halves = lax.broadcasted_iota(jnp.int32, (2, ROWS, LANES), 0)
    rows = lax.broadcasted_iota(jnp.int32, (2, ROWS, LANES), 1)
    lanes = lax.broadcasted_iota(jnp.int32, (2, ROWS, LANES), 2)
    below_z = jnp.logical_and(rows < HALO, lax.axis_index("gz") == 0)
    below_y = jnp.logical_and(halves == 1, lanes >= LANES - HALO)
    below_y = jnp.logical_and(below_y, lax.axis_index("xy") == 0)
    return jnp.where(jnp.logical_or(below_z, below_y), 0.0, STEP_RATIO)


def y_up(v):
    moved = pltpu.roll(v, LANES - 1, 2)
    other = jnp.concatenate([moved[1:], moved[:1]], axis=0)
    lanes = lax.broadcasted_iota(jnp.int32, v.shape, 2)
    return jnp.where(lanes == LANES - 1, other, moved)


def y_down(v):
    moved = pltpu.roll(v, 1, 2)
    other = jnp.concatenate([moved[1:], moved[:1]], axis=0)
    lanes = lax.broadcasted_iota(jnp.int32, v.shape, 2)
    return jnp.where(lanes == 0, other, moved)


def magnetic_planes(f, factor, i):
    rows, above = pl.ds(PAD, ROWS), pl.ds(PAD + 1, ROWS)
    ey = [f[1, i + k, :, rows, :] for k in range(GROUP + 1)]
    ez = [f[2, i + k, :, rows, :] for k in range(GROUP + 1)]
    done = []
    for k in range(GROUP):
        ex, ex_up = f[0, i + k, :, rows, :], f[0, i + k, :, above, :]
        ey_up = f[1, i + k, :, above, :]
        hx = f[3, i + k, :, rows, :] - factor * ((y_up(ez[k]) - ez[k]) - (ey_up - ey[k]))
        hy = f[4, i + k, :, rows, :] - factor * ((ex_up - ex) - (ez[k + 1] - ez[k]))
        hz = f[5, i + k, :, rows, :] - factor * ((ey[k + 1] - ey[k]) - (y_up(ex) - ex))
        done.append((hx, hy, hz))
    return done


def electric_planes(f, inverse_ref, i):
    rows, below = pl.ds(PAD, ROWS), pl.ds(PAD - 1, ROWS)
    hy = [f[4, i - 1 + k, :, rows, :] for k in range(GROUP + 1)]
    hz = [f[5, i - 1 + k, :, rows, :] for k in range(GROUP + 1)]
    done = []
    for k in range(GROUP):
        hx, hx_down = f[3, i + k, :, rows, :], f[3, i + k, :, below, :]
        hy_down = f[4, i + k, :, below, :]
        y, z = hy[k + 1], hz[k + 1]
        inverse = inverse_ref[i + k]
        ex = f[0, i + k, :, rows, :] + inverse * ((z - y_down(z)) - (y - hy_down))
        ey = f[1, i + k, :, rows, :] + inverse * ((hx - hx_down) - (z - hz[k]))
        ez = f[2, i + k, :, rows, :] + inverse * ((y - hy[k]) - (hx - y_down(hx)))
        done.append((ex, ey, ez))
    return done


def run_steps(f, factor_ref, inverse_ref, finish):
    groups = PLANES // GROUP
    rows = pl.ds(PAD, ROWS)

    def keep_magnetic(i, done):
        for k, fields in enumerate(done):
            for part, value in enumerate(fields):
                f[3 + part, i + k, :, rows, :] = value

    def keep_electric(t, i, done):
        for k, (ex, ey, ez) in enumerate(done):
            f[0, i + k, :, rows, :] = ex
            f[1, i + k, :, rows, :] = ey
            f[2, i + k, :, rows, :] = finish(t, i + k, ez)

    def body(n, carry):
        i = 1 + lax.rem(n, groups) * GROUP
        j = 1 + lax.rem(n - 1, groups) * GROUP
        magnetic = magnetic_planes(f, factor_ref[...], i)
        electric = electric_planes(f, inverse_ref, j)
        keep_magnetic(i, magnetic)
        keep_electric((n - 1) // groups, j, electric)
        return carry

    keep_magnetic(1, magnetic_planes(f, factor_ref[...], 1))
    lax.fori_loop(1, STEPS * groups, body, 0)
    last = PLANES - GROUP + 1
    keep_electric(STEPS - 1, last, electric_planes(f, inverse_ref, last))


def entry_row(vector):
    whole = vector.astype(jnp.int32)
    return jnp.concatenate([whole[i : i + 1] for i in range(SUB)], axis=1)


def one_hot(rows, index):
    ids = lax.broadcasted_iota(jnp.int32, (rows, index.shape[1]), 0)
    return jnp.where(ids == index, 1.0, 0.0).astype(BF16)


def split(values):
    high = values.astype(BF16)
    return high, (values - high.astype(F32)).astype(BF16)


def write_back(f, outs):
    me = lax.axis_index("xy")
    for m, out in enumerate(outs):
        base = (me ^ m) * CX + 1
        for part in range(6):
            for x in range(CX):
                for zt in range(ZT):
                    out[(part * CX + x) * ZT + zt] = f[
                        part, base + x, 0, pl.ds(PAD + HALO + zt * SUB, SUB), :
                    ]


def clear_edges(f):
    for part in range(6):
        for plane in (0, PLANES + 1):
            f[part, plane] = jnp.zeros(f.shape[2:], F32)
        for start in (0, PAD + ROWS):
            f[part, :, :, pl.ds(start, PAD), :] = jnp.zeros((PLANES + 2, 2, PAD, LANES), F32)


def field_put(f):
    def put(part, plane, row, columns, margins):
        rows = pl.ds(pl.multiple_of(PAD + row, SUB), SUB)
        f[part, plane, 0, rows, :] = columns
        f[part, plane, 1, rows, :] = margins

    return put


def forward_kernel(
    b0, b1, b2, b3, first_ref, second_ref, kernel_ref,
    o0, o1, o2, o3, inverse_ref, table_ref,
    f, factor_ref, record_ref, picked_ref,
):
    me = lax.axis_index("xy")
    blocks = (b0, b1, b2, b3)
    clear_edges(f)
    put_field = field_put(f)

    def put(part, plane, row, columns, margins):
        if part == 6:
            inverse_ref[plane, 0, pl.ds(row, SUB), :] = columns
            inverse_ref[plane, 1, pl.ds(row, SUB), :] = margins
        else:
            put_field(part, plane, row, columns, margins)

    unpack(7, 0, blocks, first_ref, second_ref, put)
    factor_ref[...] = magnetic_factor()

    def finish(t, i, ez):
        x = i - 1
        for part, value in enumerate(split(ez[0, HALO : HALO + CZ])):
            record_ref[x // CX, part, t, lax.rem(x, CX)] = value
        return ez

    run_steps(f, factor_ref, inverse_ref, finish)
    write_back(f, (o0, o1, o2, o3))

    bins = table_ref.shape[1]
    per_tile = CX * CZ
    copies = 2 * STEPS
    lists = ZT * packed_rows(7)
    bin_hots = []
    for m, block in enumerate(blocks):
        cells = entry_row(block[lists])
        where = jnp.where((cells // LANES) % TILES == me, cells // (LANES * TILES), -1)
        bin_hots.append(one_hot(bins, entry_row(block[lists + 1])))
        values = record_ref[me ^ m].reshape(copies * per_tile, LANES)
        for start in range(0, ENTRIES, CHUNK):
            span = slice(start, start + CHUNK)
            lane_hot = one_hot(LANES, cells[:, span] % LANES)
            row_ids = lax.broadcasted_iota(jnp.int32, (per_tile, CHUNK), 0)
            hit = row_ids == where[:, span]
            at_lane = jnp.dot(values, lane_hot, preferred_element_type=F32)
            at_lane = at_lane.reshape(copies, per_tile, CHUNK)
            picked = jnp.where(hit[None], at_lane, 0.0).astype(BF16)
            picked_ref[:, m * ENTRIES + start : m * ENTRIES + start + CHUNK] = picked.reshape(
                copies * per_tile, CHUNK
            )
    sums = lax.dot_general(
        picked_ref[...],
        jnp.concatenate(bin_hots, axis=1),
        (((1,), (1,)), ((), ())),
        preferred_element_type=F32,
    )
    table_ref[...] = jnp.dot(
        kernel_ref[...], sums, precision=lax.Precision.HIGHEST, preferred_element_type=F32
    )


def adjoint_kernel(
    b0, b1, b2, b3, first_ref, second_ref, inverse_ref, totals_ref, weight_ref, kernel_ref,
    o0, o1, o2, o3,
    f, factor_ref, drive_ref,
):
    me = lax.axis_index("xy")
    even = lax.rem(lax.axis_index("gz"), 2) == 0
    blocks = (b0, b1, b2, b3)
    clear_edges(f)
    unpack(6, 2, blocks, first_ref, second_ref, field_put(f))
    factor_ref[...] = magnetic_factor()

    totals = totals_ref[...]
    bins = totals.shape[1]
    coefficients = normalize(totals, weight_ref[...])
    by_bin = jnp.zeros((STEPS, bins), F32)
    for k in range(2 * NFREQ):
        by_bin = by_bin + kernel_ref[:, k : k + 1] * coefficients[k : k + 1, :]
    by_bin = jnp.concatenate(split(by_bin), axis=0)

    def drive(ref, start, planes, z_first, z_count, row):
        cells = entry_row(ref[start]) - 1
        bin_hot = one_hot(bins, entry_row(ref[start + 1]))
        columns = cells % (LANES * TILES) - me * LANES
        inside = jnp.logical_and(columns >= -HALO, columns < LANES + HALO)
        inside = jnp.logical_and(inside, cells >= 0)
        lane_hot = one_hot(WIDE, jnp.where(inside, columns % WIDE, -1))
        z = (cells // (LANES * TILES)) % CZ - z_first
        x = cells // (LANES * TILES * CZ)
        kept = jnp.logical_and(z >= 0, z < z_count)
        where = jnp.where(kept, x * z_count + z, -1)
        count = CX * z_count
        hit = lax.broadcasted_iota(jnp.int32, (count, ENTRIES), 0) == where
        amplitude = jnp.dot(by_bin, bin_hot, preferred_element_type=F32)
        spread = jnp.concatenate(
            [
                jnp.where(hit, amplitude[k : k + 1, :], 0.0).astype(BF16)
                for k in range(2 * STEPS)
            ],
            axis=0,
        )
        total = lax.dot_general(
            spread, lane_hot, (((1,), (1,)), ((), ())), preferred_element_type=F32
        )
        total = total[: STEPS * count] + total[STEPS * count :]
        for t in range(STEPS):
            for k in range(CX):
                at = t * count + k * z_count
                for half in range(2):
                    drive_ref[t, planes + k, half, pl.ds(row, z_count), :] = total[
                        at : at + z_count, half * LANES : (half + 1) * LANES
                    ]

    size = packed_rows(6)
    z_first = jnp.where(even, 0, HALO)
    row_first = pl.multiple_of(jnp.where(even, HALO + CZ, 0), SUB)
    row_second = pl.multiple_of(jnp.where(even, 0, HALO + CZ), SUB)
    for m, block in enumerate(blocks):
        planes = (me ^ m) * CX
        drive(block, ZT * size, planes, 0, CZ, HALO)
        drive(first_ref, m * (size + 2) + size, planes, z_first, HALO, row_first)
        drive(second_ref, m * (size + 2) + size, planes, HALO - z_first, HALO, row_second)

    run_steps(f, factor_ref, inverse_ref, lambda t, i, ez: ez + drive_ref[t, i - 1])
    write_back(f, (o0, o1, o2, o3))


def spread_kernel(b0, b1, b2, b3, out_ref):
    me = lax.axis_index("xy")
    for m, block in enumerate((b0, b1, b2, b3)):
        lane = pl.multiple_of((me ^ m) * LANES, LANES)
        for part in range(6):
            for x in range(CX):
                for zt in range(ZT):
                    out_ref[part, x, zt * SUB : (zt + 1) * SUB, pl.ds(lane, LANES)] = block[
                        (part * CX + x) * ZT + zt
                    ]


def struct(*shape):
    return jax.ShapeDtypeStruct(shape, F32)


def in_vmem(count):
    return [pl.BlockSpec(memory_space=pltpu.VMEM)] * count


def call(kernel, args, outs, scratch=(), scalars=()):
    specs = in_vmem(len(args))
    for place in scalars:
        specs[place] = pl.BlockSpec(memory_space=pltpu.SMEM)
    single = not isinstance(outs, list)
    return pl.pallas_call(
        kernel,
        out_shape=outs,
        in_specs=specs,
        out_specs=pl.BlockSpec(memory_space=pltpu.VMEM) if single else in_vmem(len(outs)),
        scratch_shapes=list(scratch),
        compiler_params=pltpu.CompilerParams(vmem_limit_bytes=48 * 1024 * 1024),
    )(*args)


def swap(value, axis, distance):
    count = lax.axis_size(axis)
    return lax.ppermute(value, axis, [(i, i ^ distance) for i in range(count)])


def swap_blocks(blocks):
    return [blocks[0]] + [swap(blocks[m], "xy", m) for m in range(1, TILES)]


def swap_neighbours(first, second):
    count = lax.axis_size("gz")
    pairs = [(i, i ^ 1) for i in range(count) if i ^ 1 < count]
    others = [(i, ((i + 1) ^ 1) - 1) for i in range(count)]
    others = [(i, j) for i, j in others if 0 <= j < count]
    return lax.ppermute(first, "gz", pairs), lax.ppermute(second, "gz", others)


def sum_all(table):
    for axis in ("xy", "gz"):
        distance = 1
        while distance < lax.axis_size(axis):
            table = table + swap(table, axis, distance)
            distance *= 2
    return table


def local_columns(
    fields,
    adjoint_fields,
    material_ids,
    material_eps,
    monitor_cells,
    monitor_bins,
    source_cells,
    source_bins,
    bin_weight,
):
    bins = bin_weight.shape[0]
    record_kernel, source_kernel = time_kernels(STEPS)
    by_row = np.tile(np.repeat(record_kernel.T, CX * CZ, axis=1), (1, 2))
    lists = [
        v.reshape(SUB, LANES) for v in (monitor_cells, monitor_bins, source_cells, source_bins)
    ]
    n_fwd, n_adj = packed_rows(7), packed_rows(6)
    sent = call(
        pack_forward_kernel,
        (fields, material_ids, material_eps, lists[0], lists[1]),
        [struct(ZT * n_fwd + 2, SUB, LANES)] * TILES,
        [pltpu.VMEM((CX, CZ, TILES * LANES), F32)],
        scalars=(2,),
    )
    adjoint_sent = call(
        pack_adjoint_kernel,
        (adjoint_fields, lists[2], lists[3]),
        [struct(ZT * n_adj + 2, SUB, LANES)] * TILES,
    )
    blocks = swap_blocks(sent)
    slabs = call(
        functools.partial(slab_kernel, n_fwd, 0), blocks, [struct(TILES * n_fwd, SUB, LANES)] * 2
    )
    slabs, adjoint_sent = lax.optimization_barrier((slabs, adjoint_sent))
    first, second = swap_neighbours(*slabs)
    adjoint_blocks = swap_blocks(adjoint_sent)
    (first, second), adjoint_blocks = lax.optimization_barrier(((first, second), adjoint_blocks))
    adjoint_slabs = call(
        functools.partial(slab_kernel, n_adj, 2),
        adjoint_blocks,
        [struct(TILES * (n_adj + 2), SUB, LANES)] * 2,
    )
    adjoint_first, adjoint_second = swap_neighbours(*adjoint_slabs)
    field = pltpu.VMEM((6, PLANES + 2, 2, ROWS + 2 * PAD, LANES), F32)
    factor = pltpu.VMEM((2, ROWS, LANES), F32)
    *forward_sent, inverse, table = call(
        forward_kernel,
        (*blocks, first, second, by_row),
        [struct(6 * CX * ZT, SUB, LANES)] * TILES
        + [struct(PLANES + 2, 2, ROWS, LANES), struct(2 * NFREQ, bins)],
        [
            field,
            factor,
            pltpu.VMEM((TILES, 2, STEPS, CX, CZ, LANES), BF16),
            pltpu.VMEM((2 * STEPS * CX * CZ, TILES * ENTRIES), BF16),
        ],
    )
    totals = sum_all(table)
    forward_blocks = swap_blocks(forward_sent)
    own_count = bins // (lax.axis_size("xy") * lax.axis_size("gz"))
    device_rank = lax.axis_index(("xy", "gz"))
    monitor_dft = lax.dynamic_slice_in_dim(totals, device_rank * own_count, own_count, axis=1)
    adjoint_back = call(
        adjoint_kernel,
        (
            *adjoint_blocks,
            adjoint_first,
            adjoint_second,
            inverse,
            totals,
            bin_weight.reshape(1, bins),
            source_kernel,
        ),
        [struct(6 * CX * ZT, SUB, LANES)] * TILES,
        [field, factor, pltpu.VMEM((STEPS, PLANES, 2, ROWS, LANES), F32)],
    )
    forward_out = call(spread_kernel, forward_blocks, struct(*fields.shape))
    adjoint_out = call(spread_kernel, swap_blocks(adjoint_back), struct(*fields.shape))
    return (forward_out, adjoint_out, monitor_dft)


def solution(mesh):
    placed = (
        P("grp", "xy", "gz", None),
        P("grp", "xy", "gz", None),
        P("xy", "gz", "grp"),
        P(),
        P("xy", "gz", "grp"),
        P("xy", "gz", "grp"),
        P("xy", "gz", "grp"),
        P("xy", "gz", "grp"),
        P("grp"),
    )
    columns = mesh.shape["xy"] == TILES and mesh.shape["gz"] & (mesh.shape["gz"] - 1) == 0
    return jax.shard_map(
        local_columns if columns else local_general,
        mesh=mesh,
        in_specs=placed,
        out_specs=(P("grp", "xy", "gz", None), P("grp", "xy", "gz", None), P("grp", ("xy", "gz"))),
        check_vma=False,
    )
```

```python
import functools

import jax
import jax.numpy as jnp
import numpy as np
from jax import lax
from jax.experimental import pallas as pl
from jax.experimental.pallas import tpu as pltpu
from jax.sharding import PartitionSpec as P

STEPS = 8
NFREQ = 4
STEP_RATIO = 0.5


def from_behind(value, axis, steps):
    count = lax.axis_size(axis)
    first, last = (max(0, -steps), min(count, count - steps))
    return lax.ppermute(value, axis, [(source, source + steps) for source in range(first, last)])


def forward_diff(values, after, along):
    upper = jnp.concatenate(
        [
            lax.slice_in_dim(values, 1, values.shape[along], axis=along),
            jnp.expand_dims(after, along),
        ],
        axis=along,
    )
    return upper - values


def backward_diff(values, before, along):
    lower = jnp.concatenate(
        [
            jnp.expand_dims(before, along),
            lax.slice_in_dim(values, 0, values.shape[along] - 1, axis=along),
        ],
        axis=along,
    )
    return values - lower


def update_magnetic(electric, magnetic):
    electric_x, electric_y, electric_z = electric
    magnetic_x, magnetic_y, magnetic_z = magnetic
    x_next = from_behind(jnp.stack([electric_y[0], electric_z[0]]), "xy", -1)
    z_next = from_behind(jnp.stack([electric_x[:, 0], electric_y[:, 0]]), "gz", -1)
    zero_y = jnp.zeros_like(electric_x[:, :, 0])
    magnetic_x = magnetic_x - STEP_RATIO * (
        forward_diff(electric_z, zero_y, 2) - forward_diff(electric_y, z_next[1], 1)
    )
    magnetic_y = magnetic_y - STEP_RATIO * (
        forward_diff(electric_x, z_next[0], 1) - forward_diff(electric_z, x_next[1], 0)
    )
    magnetic_z = magnetic_z - STEP_RATIO * (
        forward_diff(electric_y, x_next[0], 0) - forward_diff(electric_x, zero_y, 2)
    )
    return (magnetic_x, magnetic_y, magnetic_z)


def update_electric(electric, magnetic, inverse):
    electric_x, electric_y, electric_z = electric
    magnetic_x, magnetic_y, magnetic_z = magnetic
    x_prev = from_behind(jnp.stack([magnetic_y[-1], magnetic_z[-1]]), "xy", 1)
    z_prev = from_behind(jnp.stack([magnetic_x[:, -1], magnetic_y[:, -1]]), "gz", 1)
    zero_y = jnp.zeros_like(electric_x[:, :, 0])
    electric_x = electric_x + STEP_RATIO * inverse * (
        backward_diff(magnetic_z, zero_y, 2) - backward_diff(magnetic_y, z_prev[1], 1)
    )
    electric_y = electric_y + STEP_RATIO * inverse * (
        backward_diff(magnetic_x, z_prev[0], 1) - backward_diff(magnetic_z, x_prev[1], 0)
    )
    electric_z = electric_z + STEP_RATIO * inverse * (
        backward_diff(magnetic_y, x_prev[0], 0) - backward_diff(magnetic_x, zero_y, 2)
    )
    return (electric_x, electric_y, electric_z)


def inverse_permittivity(material_ids, material_eps):
    result = jnp.zeros(material_ids.shape, jnp.float32)
    for material in range(material_eps.shape[0]):
        result = jnp.where(material_ids == material, 1.0 / material_eps[material], result)
    return result


def time_kernels(count):
    times = np.arange(count) + 1.0
    omegas = 0.3 + 0.35 * np.arange(NFREQ)
    phases = times[:, None] * omegas[None, :]
    record_kernel = np.concatenate([np.cos(phases), -np.sin(phases)], axis=1)
    reverse = count - np.arange(count)
    back_phases = reverse[:, None] * omegas[None, :]
    source_kernel = np.concatenate([np.cos(back_phases), np.sin(back_phases)], axis=1)
    return (record_kernel.astype(np.float32), source_kernel.astype(np.float32))


def normalize(totals, weights):
    real_part = totals[:NFREQ]
    imag_part = totals[NFREQ:]
    scale = weights / jnp.sqrt(1.0 + real_part * real_part + imag_part * imag_part)
    return jnp.concatenate([real_part * scale, imag_part * scale], axis=0)


def local_general(
    fields,
    adjoint_fields,
    material_ids,
    material_eps,
    monitor_cells,
    monitor_bins,
    source_cells,
    source_bins,
    bin_weight,
):
    inverse = inverse_permittivity(material_ids, material_eps)
    record_kernel, source_kernel = time_kernels(STEPS)
    watched = monitor_cells.reshape(-1)
    electric = (fields[0], fields[1], fields[2])
    magnetic = (fields[3], fields[4], fields[5])
    records = []
    for _ in range(STEPS):
        magnetic = update_magnetic(electric, magnetic)
        electric = update_electric(electric, magnetic, inverse)
        records.append(electric[2].reshape(-1)[watched])
    forward_out = jnp.stack(list(electric) + list(magnetic))
    samples = jnp.stack(records)
    partial_dft = jnp.dot(samples.T, record_kernel, precision=lax.Precision.HIGHEST)
    bin_table = jax.ops.segment_sum(
        partial_dft, monitor_bins.reshape(-1), num_segments=bin_weight.shape[0]
    ).T
    owners = lax.axis_size("xy") * lax.axis_size("gz")
    own_count = bin_table.shape[1] // owners
    device_rank = lax.axis_index(("xy", "gz"))
    totals = lax.psum(bin_table, ("xy", "gz"))
    monitor_dft = lax.dynamic_slice_in_dim(totals, device_rank * own_count, own_count, axis=1)
    coefficients = normalize(totals, bin_weight[None, :])
    picked = jnp.take(coefficients, source_bins.reshape(-1), axis=1)
    amplitudes = jnp.dot(source_kernel, picked, precision=lax.Precision.HIGHEST)
    targets = source_cells.reshape(-1)
    electric = (adjoint_fields[0], adjoint_fields[1], adjoint_fields[2])
    magnetic = (adjoint_fields[3], adjoint_fields[4], adjoint_fields[5])
    for step_index in range(STEPS):
        magnetic = update_magnetic(electric, magnetic)
        electric = update_electric(electric, magnetic, inverse)
        driven = (
            electric[2]
            .reshape(-1)
            .at[targets]
            .add(amplitudes[step_index])
            .reshape(electric[2].shape)
        )
        electric = (electric[0], electric[1], driven)
    adjoint_out = jnp.stack(list(electric) + list(magnetic))
    return (forward_out, adjoint_out, monitor_dft)


TILES = 4
CX = 4
CZ = 16
LANES = 128
HALO = 8
ROWS = CZ + 2 * HALO
PAD = 8
GROUP = 2
WIDE = 2 * LANES
PLANES = TILES * CX
ENTRIES = 1024
CHUNK = 256
SUB = 8
ZT = CZ // SUB
BF16 = jnp.bfloat16
F32 = jnp.float32


def packed_rows(parts):
    return parts * CX + (parts + 1) // 2


def lane_ids():
    return lax.broadcasted_iota(jnp.int32, (SUB, LANES), 1)


def pack_block(read, regions, parts, column, store):
    lanes = lane_ids()
    upper = lanes >= LANES // 2
    take_left = jnp.logical_and(upper, column > 0)
    take_right = jnp.logical_and(jnp.logical_not(upper), column < TILES - 1)
    here = pl.multiple_of(column * LANES, LANES)
    left = pl.multiple_of(jnp.maximum(column - 1, 0) * LANES, LANES)
    right = pl.multiple_of(jnp.minimum(column + 1, TILES - 1) * LANES, LANES)
    size = packed_rows(parts)
    for zt in range(regions):
        margins = [jnp.zeros((SUB, LANES), F32) for _ in range((parts + 1) // 2)]
        for part in range(parts):
            for x in range(CX):
                store(zt * size + part * CX + x, read(part, x, zt, here))
                both = jnp.where(
                    take_left,
                    read(part, x, zt, left),
                    jnp.where(take_right, read(part, x, zt, right), 0.0),
                )
                slot = (part % 2) * CX + x
                placed = pltpu.roll(both, (16 * slot + HALO) % LANES, 1)
                margins[part // 2] = jnp.where(lanes // 16 == slot, placed, margins[part // 2])
        for pair, margin in enumerate(margins):
            store(zt * size + parts * CX + pair, margin)


def fetch(pairs, sems):
    copies = [
        pltpu.make_async_copy(source, target, sems.at[k])
        for k, (source, target) in enumerate(pairs)
    ]
    for copy in copies:
        copy.start()
    for copy in copies:
        copy.wait()


def put_list(out, row, lanes, list_ref, offset):
    for i in range(SUB):
        entries = list_ref[0, :, i * LANES : (i + 1) * LANES]
        out[row, i : i + 1, lanes] = (entries + offset).astype(F32)


def pack_forward_kernel(
    fields_hbm, ids_hbm, eps_hbm, cells_hbm, bins_hbm,
    o0, o1, o2, o3,
    fields_ref, ids_ref, eps_ref, cells_ref, bins_ref, inverse_ref, sems,
):
    me = lax.axis_index("xy")
    fetch(
        [
            (fields_hbm, fields_ref),
            (ids_hbm, ids_ref),
            (eps_hbm, eps_ref),
            (cells_hbm, cells_ref),
            (bins_hbm, bins_ref),
        ],
        sems,
    )
    ids = ids_ref[...]
    eps = jnp.full(ids.shape, eps_ref[0], F32)
    for material in range(1, eps_ref.shape[0]):
        eps = jnp.where(ids == material, eps_ref[material], eps)
    inverse_ref[...] = STEP_RATIO * (1.0 / eps)

    def read(part, x, zt, lane):
        rows = pl.ds(zt * SUB, SUB)
        if part == 6:
            return inverse_ref[x, rows, pl.ds(lane, LANES)]
        return fields_ref[part, x, rows, pl.ds(lane, LANES)]

    for m, out in enumerate((o0, o1, o2, o3)):

        def store(row, value, out=out):
            out[row] = value

        pack_block(read, ZT, 7, me ^ m, store)
        for k, ref in enumerate((cells_ref, bins_ref)):
            put_list(out, ZT * packed_rows(7) + k, slice(0, LANES), ref, 0)


def pack_adjoint_kernel(
    fields_hbm, cells_hbm, bins_hbm, weight_ref, kernel_ref,
    o0, o1, o2, o3, weight_out, kernel_out,
    fields_ref, cells_ref, bins_ref, sems,
):
    me = lax.axis_index("xy")
    fetch([(fields_hbm, fields_ref), (cells_hbm, cells_ref), (bins_hbm, bins_ref)], sems)
    weight_out[...] = weight_ref[...]
    kernel_out[...] = kernel_ref[...]

    def read(part, x, zt, lane):
        return fields_ref[part, x, pl.ds(zt * SUB, SUB), pl.ds(lane, LANES)]

    for m, out in enumerate((o0, o1, o2, o3)):

        def store(row, value, out=out):
            out[row] = value

        pack_block(read, ZT, 6, me ^ m, store)
        put_list(out, ZT * packed_rows(6), slice(0, LANES), cells_ref, 1)
        put_list(out, ZT * packed_rows(6) + 1, slice(0, LANES), bins_ref, 0)


def slab_kernel(parts, lists, b0, b1, b2, b3, first_ref, second_ref):
    size = packed_rows(parts)
    zt_first = jnp.where(lax.rem(lax.axis_index("gz"), 2) == 0, 1, 0)
    for m, block in enumerate((b0, b1, b2, b3)):
        base = m * (size + lists)
        first_ref[pl.ds(base, size)] = block[pl.ds(zt_first * size, size)]
        second_ref[pl.ds(base, size)] = block[pl.ds((1 - zt_first) * size, size)]
        for k in range(lists):
            first_ref[base + size + k] = block[ZT * size + k]
            second_ref[base + size + k] = block[ZT * size + k]


def edge_rows():
    even = lax.rem(lax.axis_index("gz"), 2) == 0
    return (
        pl.multiple_of(jnp.where(even, HALO + CZ, 0), SUB),
        pl.multiple_of(jnp.where(even, 0, HALO + CZ), SUB),
    )


def unpack(parts, sources, put):
    lanes = lane_ids()
    in_margin = jnp.logical_or(lanes < HALO, lanes >= LANES - HALO)
    for ref, start, row in sources:
        for part in range(parts):
            for x in range(CX):
                slot = (part % 2) * CX + x
                margin = pltpu.roll(
                    ref[start + parts * CX + part // 2], (-16 * slot - HALO) % LANES, 1
                )
                put(
                    part,
                    x,
                    row,
                    ref[start + part * CX + x],
                    jnp.where(in_margin, margin, 0.0),
                )


def magnetic_factor():
    halves = lax.broadcasted_iota(jnp.int32, (2, ROWS, LANES), 0)
    rows = lax.broadcasted_iota(jnp.int32, (2, ROWS, LANES), 1)
    lanes = lax.broadcasted_iota(jnp.int32, (2, ROWS, LANES), 2)
    below_z = jnp.logical_and(rows < HALO, lax.axis_index("gz") == 0)
    below_y = jnp.logical_and(halves == 1, lanes >= LANES - HALO)
    below_y = jnp.logical_and(below_y, lax.axis_index("xy") == 0)
    return jnp.where(jnp.logical_or(below_z, below_y), 0.0, STEP_RATIO)


def y_up(v):
    moved = pltpu.roll(v, LANES - 1, 2)
    other = jnp.concatenate([moved[1:], moved[:1]], axis=0)
    lanes = lax.broadcasted_iota(jnp.int32, v.shape, 2)
    return jnp.where(lanes == LANES - 1, other, moved)


def y_down(v):
    moved = pltpu.roll(v, 1, 2)
    other = jnp.concatenate([moved[1:], moved[:1]], axis=0)
    lanes = lax.broadcasted_iota(jnp.int32, v.shape, 2)
    return jnp.where(lanes == 0, other, moved)


def magnetic_planes(f, factor, i):
    rows, above = pl.ds(PAD, ROWS), pl.ds(PAD + 1, ROWS)
    ey = [f[1, i + k, :, rows, :] for k in range(GROUP + 1)]
    ez = [f[2, i + k, :, rows, :] for k in range(GROUP + 1)]
    done = []
    for k in range(GROUP):
        ex, ex_up = f[0, i + k, :, rows, :], f[0, i + k, :, above, :]
        ey_up = f[1, i + k, :, above, :]
        hx = f[3, i + k, :, rows, :] - factor * ((y_up(ez[k]) - ez[k]) - (ey_up - ey[k]))
        hy = f[4, i + k, :, rows, :] - factor * ((ex_up - ex) - (ez[k + 1] - ez[k]))
        hz = f[5, i + k, :, rows, :] - factor * ((ey[k + 1] - ey[k]) - (y_up(ex) - ex))
        done.append((hx, hy, hz))
    return done


def electric_planes(f, inverse_ref, i):
    rows, below = pl.ds(PAD, ROWS), pl.ds(PAD - 1, ROWS)
    hy = [f[4, i - 1 + k, :, rows, :] for k in range(GROUP + 1)]
    hz = [f[5, i - 1 + k, :, rows, :] for k in range(GROUP + 1)]
    done = []
    for k in range(GROUP):
        hx, hx_down = f[3, i + k, :, rows, :], f[3, i + k, :, below, :]
        hy_down = f[4, i + k, :, below, :]
        y, z = hy[k + 1], hz[k + 1]
        inverse = inverse_ref[i + k]
        ex = f[0, i + k, :, rows, :] + inverse * ((z - y_down(z)) - (y - hy_down))
        ey = f[1, i + k, :, rows, :] + inverse * ((hx - hx_down) - (z - hz[k]))
        ez = f[2, i + k, :, rows, :] + inverse * ((y - hy[k]) - (hx - y_down(hx)))
        done.append((ex, ey, ez))
    return done


def run_steps(f, factor_ref, inverse_ref, finish):
    rows = pl.ds(PAD, ROWS)

    def body(t, carry):
        for i in range(1, PLANES + 2, GROUP):
            magnetic = magnetic_planes(f, factor_ref[...], i) if i <= PLANES else []
            electric = electric_planes(f, inverse_ref, i - GROUP) if i > 1 else []
            for k, fields in enumerate(magnetic):
                for part, value in enumerate(fields):
                    f[3 + part, i + k, :, rows, :] = value
            for k, (ex, ey, ez) in enumerate(electric):
                j = i - GROUP + k
                f[0, j, :, rows, :] = ex
                f[1, j, :, rows, :] = ey
                f[2, j, :, rows, :] = finish(t, j, ez)
        return carry

    lax.fori_loop(0, STEPS, body, 0)


def entry_row(vector):
    whole = vector.astype(jnp.int32)
    return jnp.concatenate([whole[i : i + 1] for i in range(SUB)], axis=1)


def one_hot(rows, index):
    ids = lax.broadcasted_iota(jnp.int32, (rows, index.shape[1]), 0)
    return jnp.where(ids == index, 1.0, 0.0).astype(BF16)


def split(values):
    high = values.astype(BF16)
    return high, (values - high.astype(F32)).astype(BF16)


def write_back(f, outs):
    me = lax.axis_index("xy")
    for m, out in enumerate(outs):
        base = (me ^ m) * CX + 1
        for part in range(6):
            for x in range(CX):
                for zt in range(ZT):
                    out[(part * CX + x) * ZT + zt] = f[
                        part, base + x, 0, pl.ds(PAD + HALO + zt * SUB, SUB), :
                    ]


def clear_edges(f):
    for part in range(6):
        for plane in (0, PLANES + 1):
            f[part, plane] = jnp.zeros(f.shape[2:], F32)
        for start in (0, PAD + ROWS):
            f[part, :, :, pl.ds(start, PAD), :] = jnp.zeros((PLANES + 2, 2, PAD, LANES), F32)


def field_put(f, base):
    def put(part, x, row, columns, margins):
        plane = base + x
        rows = pl.ds(pl.multiple_of(PAD + row, SUB), SUB)
        f[part, plane, 0, rows, :] = columns
        f[part, plane, 1, rows, :] = margins

    return put


def forward_kernel(
    b0, b1, b2, b3, first_ref, second_ref, kernel_ref,
    o0, o1, o2, o3, inverse_ref, table_ref,
    f, factor_ref, record_ref, picked_ref,
):
    me = lax.axis_index("xy")
    blocks = (b0, b1, b2, b3)
    clear_edges(f)
    row_first, row_second = edge_rows()
    size = packed_rows(7)
    for m, block in enumerate(blocks):
        base = (me ^ m) * CX + 1
        put_field = field_put(f, base)

        def put(part, x, row, columns, margins, base=base, put_field=put_field):
            if part == 6:
                inverse_ref[base + x, 0, pl.ds(row, SUB), :] = columns
                inverse_ref[base + x, 1, pl.ds(row, SUB), :] = margins
            else:
                put_field(part, x, row, columns, margins)

        sources = [
            (first_ref, m * size, row_first),
            (second_ref, m * size, row_second),
            (block, 0, HALO),
            (block, size, HALO + SUB),
        ]
        unpack(7, sources, put)
    factor_ref[...] = magnetic_factor()

    def finish(t, i, ez):
        x = i - 1
        for part, value in enumerate(split(ez[0, HALO : HALO + CZ])):
            record_ref[x // CX, part, t, x % CX] = value
        return ez

    run_steps(f, factor_ref, inverse_ref, finish)
    write_back(f, (o0, o1, o2, o3))

    bins = table_ref.shape[1]
    per_tile = CX * CZ
    copies = 2 * STEPS
    lists = ZT * packed_rows(7)
    bin_hots = []
    for m, block in enumerate(blocks):
        cells = entry_row(block[lists])
        where = jnp.where((cells // LANES) % TILES == me, cells // (LANES * TILES), -1)
        bin_hots.append(one_hot(bins, entry_row(block[lists + 1])))
        values = record_ref[me ^ m].reshape(copies * per_tile, LANES)
        for start in range(0, ENTRIES, CHUNK):
            span = slice(start, start + CHUNK)
            lane_hot = one_hot(LANES, cells[:, span] % LANES)
            row_ids = lax.broadcasted_iota(jnp.int32, (per_tile, CHUNK), 0)
            hit = row_ids == where[:, span]
            at_lane = jnp.dot(values, lane_hot, preferred_element_type=F32)
            at_lane = at_lane.reshape(copies, per_tile, CHUNK)
            picked = jnp.where(hit[None], at_lane, 0.0).astype(BF16)
            picked_ref[:, m * ENTRIES + start : m * ENTRIES + start + CHUNK] = picked.reshape(
                copies * per_tile, CHUNK
            )
    sums = lax.dot_general(
        picked_ref[...],
        jnp.concatenate(bin_hots, axis=1),
        (((1,), (1,)), ((), ())),
        preferred_element_type=F32,
    )
    table_ref[...] = jnp.dot(
        kernel_ref[...], sums, precision=lax.Precision.HIGHEST, preferred_element_type=F32
    )


def adjoint_kernel(
    b0, b1, b2, b3, first_ref, second_ref, inverse_ref, totals_ref, weight_ref, kernel_ref,
    o0, o1, o2, o3,
    f, factor_ref, drive_ref,
):
    me = lax.axis_index("xy")
    even = lax.rem(lax.axis_index("gz"), 2) == 0
    blocks = (b0, b1, b2, b3)
    clear_edges(f)
    row_first, row_second = edge_rows()
    size = packed_rows(6)
    for m, block in enumerate(blocks):
        sources = [
            (first_ref, m * (size + 2), row_first),
            (second_ref, m * (size + 2), row_second),
            (block, 0, HALO),
            (block, size, HALO + SUB),
        ]
        unpack(6, sources, field_put(f, (me ^ m) * CX + 1))
    factor_ref[...] = magnetic_factor()

    totals = totals_ref[...]
    bins = totals.shape[1]
    coefficients = normalize(totals, weight_ref[...])
    by_bin = jnp.zeros((STEPS, bins), F32)
    for k in range(2 * NFREQ):
        by_bin = by_bin + kernel_ref[:, k : k + 1] * coefficients[k : k + 1, :]
    by_bin = jnp.concatenate(split(by_bin), axis=0)

    def drive(ref, start, planes, z_first, z_count, row):
        cells = entry_row(ref[start]) - 1
        bin_hot = one_hot(bins, entry_row(ref[start + 1]))
        columns = cells % (LANES * TILES) - me * LANES
        inside = jnp.logical_and(columns >= -HALO, columns < LANES + HALO)
        inside = jnp.logical_and(inside, cells >= 0)
        lane_hot = one_hot(WIDE, jnp.where(inside, columns % WIDE, -1))
        z = (cells // (LANES * TILES)) % CZ - z_first
        x = cells // (LANES * TILES * CZ)
        kept = jnp.logical_and(z >= 0, z < z_count)
        where = jnp.where(kept, x * z_count + z, -1)
        count = CX * z_count
        hit = lax.broadcasted_iota(jnp.int32, (count, ENTRIES), 0) == where
        amplitude = jnp.dot(by_bin, bin_hot, preferred_element_type=F32)
        spread = jnp.concatenate(
            [
                jnp.where(hit, amplitude[k : k + 1, :], 0.0).astype(BF16)
                for k in range(2 * STEPS)
            ],
            axis=0,
        )
        total = lax.dot_general(
            spread, lane_hot, (((1,), (1,)), ((), ())), preferred_element_type=F32
        )
        total = total[: STEPS * count] + total[STEPS * count :]
        for t in range(STEPS):
            for k in range(CX):
                at = t * count + k * z_count
                for half in range(2):
                    drive_ref[t, planes + k, half, pl.ds(row, z_count), :] = total[
                        at : at + z_count, half * LANES : (half + 1) * LANES
                    ]

    z_first = jnp.where(even, 0, HALO)
    for m, block in enumerate(blocks):
        planes = (me ^ m) * CX
        base = m * (size + 2) + size
        drive(block, ZT * size, planes, 0, CZ, HALO)
        drive(first_ref, base, planes, z_first, HALO, row_first)
        drive(second_ref, base, planes, HALO - z_first, HALO, row_second)

    run_steps(f, factor_ref, inverse_ref, lambda t, i, ez: ez + drive_ref[t, i - 1])
    write_back(f, (o0, o1, o2, o3))


def spread_kernel(b0, b1, b2, b3, out_ref):
    me = lax.axis_index("xy")
    for m, block in enumerate((b0, b1, b2, b3)):
        lane = pl.multiple_of((me ^ m) * LANES, LANES)
        for part in range(6):
            for x in range(CX):
                for zt in range(ZT):
                    out_ref[part, x, zt * SUB : (zt + 1) * SUB, pl.ds(lane, LANES)] = block[
                        (part * CX + x) * ZT + zt
                    ]


def struct(*shape):
    return jax.ShapeDtypeStruct(shape, F32)


def call(kernel, args, outs, scratch=(), places=None, limit=48 * 1024 * 1024):
    spaces = places or {}
    return pl.pallas_call(
        kernel,
        out_shape=outs,
        in_specs=[
            pl.BlockSpec(memory_space=spaces.get(k, pltpu.VMEM)) for k in range(len(args))
        ],
        out_specs=jax.tree.map(lambda _: pl.BlockSpec(memory_space=pltpu.VMEM), outs),
        scratch_shapes=list(scratch),
        compiler_params=pltpu.CompilerParams(vmem_limit_bytes=limit),
    )(*args)


def swap(value, axis, distance):
    count = lax.axis_size(axis)
    return lax.ppermute(value, axis, [(i, i ^ distance) for i in range(count)])


def swap_blocks(blocks):
    return [blocks[0]] + [swap(blocks[m], "xy", m) for m in range(1, TILES)]


def swap_neighbours(first, second):
    count = lax.axis_size("gz")
    pairs = [(i, i ^ 1) for i in range(count) if i ^ 1 < count]
    others = [(i, ((i + 1) ^ 1) - 1) for i in range(count)]
    others = [(i, j) for i, j in others if 0 <= j < count]
    return lax.ppermute(first, "gz", pairs), lax.ppermute(second, "gz", others)


def sum_over(table, axis):
    terms = [table] + [swap(table, axis, m) for m in range(1, lax.axis_size(axis))]
    while len(terms) > 1:
        terms = [a + b for a, b in zip(terms[::2], terms[1::2])]
    return terms[0]


def local_columns(
    fields,
    adjoint_fields,
    material_ids,
    material_eps,
    monitor_cells,
    monitor_bins,
    source_cells,
    source_bins,
    bin_weight,
):
    bins = bin_weight.shape[0]
    record_kernel, source_kernel = time_kernels(STEPS)
    by_row = np.tile(np.repeat(record_kernel.T, CX * CZ, axis=1), (1, 2))
    n_fwd, n_adj = packed_rows(7), packed_rows(6)
    hbm = pltpu.HBM
    listed = pltpu.VMEM(monitor_cells.shape, jnp.int32)
    sent = call(
        pack_forward_kernel,
        (fields, material_ids, material_eps, monitor_cells, monitor_bins),
        [struct(ZT * n_fwd + 2, SUB, LANES)] * TILES,
        [
            pltpu.VMEM(fields.shape, F32),
            pltpu.VMEM(material_ids.shape, jnp.int32),
            pltpu.SMEM(material_eps.shape, F32),
            listed,
            listed,
            pltpu.VMEM(material_ids.shape, F32),
            pltpu.SemaphoreType.DMA((5,)),
        ],
        places={k: hbm for k in range(5)},
        limit=None,
    )
    *adjoint_sent, weight, back_kernel = call(
        pack_adjoint_kernel,
        (adjoint_fields, source_cells, source_bins, bin_weight.reshape(1, bins), source_kernel),
        [struct(ZT * n_adj + 2, SUB, LANES)] * TILES
        + [struct(1, bins), struct(STEPS, 2 * NFREQ)],
        [pltpu.VMEM(fields.shape, F32), listed, listed, pltpu.SemaphoreType.DMA((3,))],
        places={k: hbm for k in range(3)},
        limit=None,
    )
    blocks = swap_blocks(sent)
    slabs = call(
        functools.partial(slab_kernel, 7, 0), blocks, [struct(TILES * n_fwd, SUB, LANES)] * 2
    )
    slabs, adjoint_sent = lax.optimization_barrier((slabs, adjoint_sent))
    first, second = swap_neighbours(*slabs)
    adjoint_blocks = swap_blocks(adjoint_sent)
    (first, second), adjoint_blocks = lax.optimization_barrier(((first, second), adjoint_blocks))
    adjoint_slabs = call(
        functools.partial(slab_kernel, 6, 2),
        adjoint_blocks,
        [struct(TILES * (n_adj + 2), SUB, LANES)] * 2,
    )
    adjoint_edges = swap_neighbours(*adjoint_slabs)
    field = pltpu.VMEM((6, PLANES + 2, 2, ROWS + 2 * PAD, LANES), F32)
    factor = pltpu.VMEM((2, ROWS, LANES), F32)
    *forward_sent, inverse, table = call(
        forward_kernel,
        (*blocks, first, second, by_row),
        [struct(6 * CX * ZT, SUB, LANES)] * TILES
        + [struct(PLANES + 2, 2, ROWS, LANES), struct(2 * NFREQ, bins)],
        [
            field,
            factor,
            pltpu.VMEM((TILES, 2, STEPS, CX, CZ, LANES), BF16),
            pltpu.VMEM((2 * STEPS * CX * CZ, TILES * ENTRIES), BF16),
        ],
    )
    table, forward_sent = lax.optimization_barrier((sum_over(table, "xy"), forward_sent))
    totals = sum_over(table, "gz")
    forward_blocks = swap_blocks(forward_sent)
    own_count = bins // (lax.axis_size("xy") * lax.axis_size("gz"))
    device_rank = lax.axis_index(("xy", "gz"))
    monitor_dft = lax.dynamic_slice_in_dim(totals, device_rank * own_count, own_count, axis=1)
    adjoint_back = call(
        adjoint_kernel,
        (
            *adjoint_blocks,
            *adjoint_edges,
            inverse,
            totals,
            weight,
            back_kernel,
        ),
        [struct(6 * CX * ZT, SUB, LANES)] * TILES,
        [field, factor, pltpu.VMEM((STEPS, PLANES, 2, ROWS, LANES), F32)],
    )
    forward_out = call(spread_kernel, forward_blocks, struct(*fields.shape))
    adjoint_out = call(spread_kernel, swap_blocks(adjoint_back), struct(*fields.shape))
    return (forward_out, adjoint_out, monitor_dft)


def solution(mesh):
    placed = (
        P("grp", "xy", "gz", None),
        P("grp", "xy", "gz", None),
        P("xy", "gz", "grp"),
        P(),
        P("xy", "gz", "grp"),
        P("xy", "gz", "grp"),
        P("xy", "gz", "grp"),
        P("xy", "gz", "grp"),
        P("grp"),
    )
    columns = mesh.shape["xy"] == TILES and mesh.shape["gz"] & (mesh.shape["gz"] - 1) == 0
    return jax.shard_map(
        local_columns if columns else local_general,
        mesh=mesh,
        in_specs=placed,
        out_specs=(P("grp", "xy", "gz", None), P("grp", "xy", "gz", None), P("grp", ("xy", "gz"))),
        check_vma=False,
    )
```

```python
import functools

import jax
import jax.numpy as jnp
import numpy as np
from jax import lax
from jax.experimental import pallas as pl
from jax.experimental.pallas import tpu as pltpu
from jax.sharding import PartitionSpec as P

STEPS = 8
NFREQ = 4
STEP_RATIO = 0.5


def from_behind(value, axis, steps):
    count = lax.axis_size(axis)
    first, last = (max(0, -steps), min(count, count - steps))
    return lax.ppermute(value, axis, [(source, source + steps) for source in range(first, last)])


def forward_diff(values, after, along):
    upper = jnp.concatenate(
        [
            lax.slice_in_dim(values, 1, values.shape[along], axis=along),
            jnp.expand_dims(after, along),
        ],
        axis=along,
    )
    return upper - values


def backward_diff(values, before, along):
    lower = jnp.concatenate(
        [
            jnp.expand_dims(before, along),
            lax.slice_in_dim(values, 0, values.shape[along] - 1, axis=along),
        ],
        axis=along,
    )
    return values - lower


def update_magnetic(electric, magnetic):
    electric_x, electric_y, electric_z = electric
    magnetic_x, magnetic_y, magnetic_z = magnetic
    x_next = from_behind(jnp.stack([electric_y[0], electric_z[0]]), "xy", -1)
    z_next = from_behind(jnp.stack([electric_x[:, 0], electric_y[:, 0]]), "gz", -1)
    zero_y = jnp.zeros_like(electric_x[:, :, 0])
    magnetic_x = magnetic_x - STEP_RATIO * (
        forward_diff(electric_z, zero_y, 2) - forward_diff(electric_y, z_next[1], 1)
    )
    magnetic_y = magnetic_y - STEP_RATIO * (
        forward_diff(electric_x, z_next[0], 1) - forward_diff(electric_z, x_next[1], 0)
    )
    magnetic_z = magnetic_z - STEP_RATIO * (
        forward_diff(electric_y, x_next[0], 0) - forward_diff(electric_x, zero_y, 2)
    )
    return (magnetic_x, magnetic_y, magnetic_z)


def update_electric(electric, magnetic, inverse):
    electric_x, electric_y, electric_z = electric
    magnetic_x, magnetic_y, magnetic_z = magnetic
    x_prev = from_behind(jnp.stack([magnetic_y[-1], magnetic_z[-1]]), "xy", 1)
    z_prev = from_behind(jnp.stack([magnetic_x[:, -1], magnetic_y[:, -1]]), "gz", 1)
    zero_y = jnp.zeros_like(electric_x[:, :, 0])
    electric_x = electric_x + STEP_RATIO * inverse * (
        backward_diff(magnetic_z, zero_y, 2) - backward_diff(magnetic_y, z_prev[1], 1)
    )
    electric_y = electric_y + STEP_RATIO * inverse * (
        backward_diff(magnetic_x, z_prev[0], 1) - backward_diff(magnetic_z, x_prev[1], 0)
    )
    electric_z = electric_z + STEP_RATIO * inverse * (
        backward_diff(magnetic_y, x_prev[0], 0) - backward_diff(magnetic_x, zero_y, 2)
    )
    return (electric_x, electric_y, electric_z)


def inverse_permittivity(material_ids, material_eps):
    result = jnp.zeros(material_ids.shape, jnp.float32)
    for material in range(material_eps.shape[0]):
        result = jnp.where(material_ids == material, 1.0 / material_eps[material], result)
    return result


def time_kernels(count):
    times = np.arange(count) + 1.0
    omegas = 0.3 + 0.35 * np.arange(NFREQ)
    phases = times[:, None] * omegas[None, :]
    record_kernel = np.concatenate([np.cos(phases), -np.sin(phases)], axis=1)
    reverse = count - np.arange(count)
    back_phases = reverse[:, None] * omegas[None, :]
    source_kernel = np.concatenate([np.cos(back_phases), np.sin(back_phases)], axis=1)
    return (record_kernel.astype(np.float32), source_kernel.astype(np.float32))


def normalize(totals, weights):
    real_part = totals[:NFREQ]
    imag_part = totals[NFREQ:]
    scale = weights / jnp.sqrt(1.0 + real_part * real_part + imag_part * imag_part)
    return jnp.concatenate([real_part * scale, imag_part * scale], axis=0)


def local_general(
    fields,
    adjoint_fields,
    material_ids,
    material_eps,
    monitor_cells,
    monitor_bins,
    source_cells,
    source_bins,
    bin_weight,
):
    inverse = inverse_permittivity(material_ids, material_eps)
    record_kernel, source_kernel = time_kernels(STEPS)
    watched = monitor_cells.reshape(-1)
    electric = (fields[0], fields[1], fields[2])
    magnetic = (fields[3], fields[4], fields[5])
    records = []
    for _ in range(STEPS):
        magnetic = update_magnetic(electric, magnetic)
        electric = update_electric(electric, magnetic, inverse)
        records.append(electric[2].reshape(-1)[watched])
    forward_out = jnp.stack(list(electric) + list(magnetic))
    samples = jnp.stack(records)
    partial_dft = jnp.dot(samples.T, record_kernel, precision=lax.Precision.HIGHEST)
    bin_table = jax.ops.segment_sum(
        partial_dft, monitor_bins.reshape(-1), num_segments=bin_weight.shape[0]
    ).T
    owners = lax.axis_size("xy") * lax.axis_size("gz")
    own_count = bin_table.shape[1] // owners
    device_rank = lax.axis_index(("xy", "gz"))
    totals = lax.psum(bin_table, ("xy", "gz"))
    monitor_dft = lax.dynamic_slice_in_dim(totals, device_rank * own_count, own_count, axis=1)
    coefficients = normalize(totals, bin_weight[None, :])
    picked = jnp.take(coefficients, source_bins.reshape(-1), axis=1)
    amplitudes = jnp.dot(source_kernel, picked, precision=lax.Precision.HIGHEST)
    targets = source_cells.reshape(-1)
    electric = (adjoint_fields[0], adjoint_fields[1], adjoint_fields[2])
    magnetic = (adjoint_fields[3], adjoint_fields[4], adjoint_fields[5])
    for step_index in range(STEPS):
        magnetic = update_magnetic(electric, magnetic)
        electric = update_electric(electric, magnetic, inverse)
        driven = (
            electric[2]
            .reshape(-1)
            .at[targets]
            .add(amplitudes[step_index])
            .reshape(electric[2].shape)
        )
        electric = (electric[0], electric[1], driven)
    adjoint_out = jnp.stack(list(electric) + list(magnetic))
    return (forward_out, adjoint_out, monitor_dft)


TILES = 4
CX = 4
CZ = 16
LANES = 128
HALO = 8
ROWS = CZ + 2 * HALO
PAD = 8
GROUP = 2
WIDE = 2 * LANES
PLANES = TILES * CX
ENTRIES = 1024
CHUNK = 256
SUB = 8
ZT = CZ // SUB
BF16 = jnp.bfloat16
F32 = jnp.float32


def packed_rows(parts):
    return parts * CX + (parts + 1) // 2


def lane_ids():
    return lax.broadcasted_iota(jnp.int32, (SUB, LANES), 1)


def pack_block(read, regions, parts, column, store):
    lanes = lane_ids()
    upper = lanes >= LANES // 2
    take_left = jnp.logical_and(upper, column > 0)
    take_right = jnp.logical_and(jnp.logical_not(upper), column < TILES - 1)
    here = pl.multiple_of(column * LANES, LANES)
    left = pl.multiple_of(jnp.maximum(column - 1, 0) * LANES, LANES)
    right = pl.multiple_of(jnp.minimum(column + 1, TILES - 1) * LANES, LANES)
    size = packed_rows(parts)
    for zt in range(regions):
        margins = [jnp.zeros((SUB, LANES), F32) for _ in range((parts + 1) // 2)]
        for part in range(parts):
            for x in range(CX):
                store(zt * size + part * CX + x, read(part, x, zt, here))
                both = jnp.where(
                    take_left,
                    read(part, x, zt, left),
                    jnp.where(take_right, read(part, x, zt, right), 0.0),
                )
                slot = (part % 2) * CX + x
                placed = pltpu.roll(both, (16 * slot + HALO) % LANES, 1)
                margins[part // 2] = jnp.where(lanes // 16 == slot, placed, margins[part // 2])
        for pair, margin in enumerate(margins):
            store(zt * size + parts * CX + pair, margin)


def fetch(pairs, sems):
    copies = [
        pltpu.make_async_copy(source, target, sems.at[k])
        for k, (source, target) in enumerate(pairs)
    ]
    for copy in copies:
        copy.start()
    for copy in copies:
        copy.wait()


def put_list(out, row, lanes, list_ref, offset):
    for i in range(SUB):
        entries = list_ref[0, :, i * LANES : (i + 1) * LANES]
        out[row, i : i + 1, lanes] = (entries + offset).astype(F32)


def pack_forward_kernel(
    fields_hbm, ids_hbm, eps_hbm, cells_hbm, bins_hbm,
    o0, o1, o2, o3,
    fields_ref, ids_ref, eps_ref, cells_ref, bins_ref, inverse_ref, sems,
):
    me = lax.axis_index("xy")
    fetch(
        [
            (fields_hbm, fields_ref),
            (ids_hbm, ids_ref),
            (eps_hbm, eps_ref),
            (cells_hbm, cells_ref),
            (bins_hbm, bins_ref),
        ],
        sems,
    )
    ids = ids_ref[...]
    eps = jnp.full(ids.shape, eps_ref[0], F32)
    for material in range(1, eps_ref.shape[0]):
        eps = jnp.where(ids == material, eps_ref[material], eps)
    inverse_ref[...] = STEP_RATIO * (1.0 / eps)

    def read(part, x, zt, lane):
        rows = pl.ds(zt * SUB, SUB)
        if part == 6:
            return inverse_ref[x, rows, pl.ds(lane, LANES)]
        return fields_ref[part, x, rows, pl.ds(lane, LANES)]

    for m, out in enumerate((o0, o1, o2, o3)):

        def store(row, value, out=out):
            out[row] = value

        pack_block(read, ZT, 7, me ^ m, store)
        for k, ref in enumerate((cells_ref, bins_ref)):
            put_list(out, ZT * packed_rows(7) + k, slice(0, LANES), ref, 0)


def pack_adjoint_kernel(
    fields_hbm, cells_hbm, bins_hbm, weight_ref, kernel_ref,
    o0, o1, o2, o3, weight_out, kernel_out,
    fields_ref, cells_ref, bins_ref, sems,
):
    me = lax.axis_index("xy")
    fetch([(fields_hbm, fields_ref), (cells_hbm, cells_ref), (bins_hbm, bins_ref)], sems)
    weight_out[...] = weight_ref[...]
    kernel_out[...] = kernel_ref[...]

    def read(part, x, zt, lane):
        return fields_ref[part, x, pl.ds(zt * SUB, SUB), pl.ds(lane, LANES)]

    for m, out in enumerate((o0, o1, o2, o3)):

        def store(row, value, out=out):
            out[row] = value

        pack_block(read, ZT, 6, me ^ m, store)
        put_list(out, ZT * packed_rows(6), slice(0, LANES), cells_ref, 1)
        put_list(out, ZT * packed_rows(6) + 1, slice(0, LANES), bins_ref, 0)


def slab_kernel(parts, lists, b0, b1, b2, b3, first_ref, second_ref):
    size = packed_rows(parts)
    zt_first = jnp.where(lax.rem(lax.axis_index("gz"), 2) == 0, 1, 0)
    for m, block in enumerate((b0, b1, b2, b3)):
        base = m * (size + lists)
        first_ref[pl.ds(base, size)] = block[pl.ds(zt_first * size, size)]
        second_ref[pl.ds(base, size)] = block[pl.ds((1 - zt_first) * size, size)]
        for k in range(lists):
            first_ref[base + size + k] = block[ZT * size + k]
            second_ref[base + size + k] = block[ZT * size + k]


def edge_rows():
    even = lax.rem(lax.axis_index("gz"), 2) == 0
    return (
        pl.multiple_of(jnp.where(even, HALO + CZ, 0), SUB),
        pl.multiple_of(jnp.where(even, 0, HALO + CZ), SUB),
    )


def unpack(parts, sources, put):
    lanes = lane_ids()
    in_margin = jnp.logical_or(lanes < HALO, lanes >= LANES - HALO)
    for ref, start, row in sources:
        for part in range(parts):
            for x in range(CX):
                slot = (part % 2) * CX + x
                margin = pltpu.roll(
                    ref[start + parts * CX + part // 2], (-16 * slot - HALO) % LANES, 1
                )
                put(
                    part,
                    x,
                    row,
                    ref[start + part * CX + x],
                    jnp.where(in_margin, margin, 0.0),
                )


def magnetic_factor():
    halves = lax.broadcasted_iota(jnp.int32, (2, ROWS, LANES), 0)
    rows = lax.broadcasted_iota(jnp.int32, (2, ROWS, LANES), 1)
    lanes = lax.broadcasted_iota(jnp.int32, (2, ROWS, LANES), 2)
    below_z = jnp.logical_and(rows < HALO, lax.axis_index("gz") == 0)
    below_y = jnp.logical_and(halves == 1, lanes >= LANES - HALO)
    below_y = jnp.logical_and(below_y, lax.axis_index("xy") == 0)
    return jnp.where(jnp.logical_or(below_z, below_y), 0.0, STEP_RATIO)


def y_up(v):
    moved = pltpu.roll(v, LANES - 1, 2)
    other = jnp.concatenate([moved[1:], moved[:1]], axis=0)
    lanes = lax.broadcasted_iota(jnp.int32, v.shape, 2)
    return jnp.where(lanes == LANES - 1, other, moved)


def y_down(v):
    moved = pltpu.roll(v, 1, 2)
    other = jnp.concatenate([moved[1:], moved[:1]], axis=0)
    lanes = lax.broadcasted_iota(jnp.int32, v.shape, 2)
    return jnp.where(lanes == 0, other, moved)


def magnetic_planes(f, factor, i):
    rows, above = pl.ds(PAD, ROWS), pl.ds(PAD + 1, ROWS)
    ey = [f[1, i + k, :, rows, :] for k in range(GROUP + 1)]
    ez = [f[2, i + k, :, rows, :] for k in range(GROUP + 1)]
    done = []
    for k in range(GROUP):
        ex, ex_up = f[0, i + k, :, rows, :], f[0, i + k, :, above, :]
        ey_up = f[1, i + k, :, above, :]
        hx = f[3, i + k, :, rows, :] - factor * ((y_up(ez[k]) - ez[k]) - (ey_up - ey[k]))
        hy = f[4, i + k, :, rows, :] - factor * ((ex_up - ex) - (ez[k + 1] - ez[k]))
        hz = f[5, i + k, :, rows, :] - factor * ((ey[k + 1] - ey[k]) - (y_up(ex) - ex))
        done.append((hx, hy, hz))
    return done


def electric_planes(f, inverse_ref, i):
    rows, below = pl.ds(PAD, ROWS), pl.ds(PAD - 1, ROWS)
    hy = [f[4, i - 1 + k, :, rows, :] for k in range(GROUP + 1)]
    hz = [f[5, i - 1 + k, :, rows, :] for k in range(GROUP + 1)]
    done = []
    for k in range(GROUP):
        hx, hx_down = f[3, i + k, :, rows, :], f[3, i + k, :, below, :]
        hy_down = f[4, i + k, :, below, :]
        y, z = hy[k + 1], hz[k + 1]
        inverse = inverse_ref[i + k]
        ex = f[0, i + k, :, rows, :] + inverse * ((z - y_down(z)) - (y - hy_down))
        ey = f[1, i + k, :, rows, :] + inverse * ((hx - hx_down) - (z - hz[k]))
        ez = f[2, i + k, :, rows, :] + inverse * ((y - hy[k]) - (hx - y_down(hx)))
        done.append((ex, ey, ez))
    return done


def run_steps(f, factor_ref, inverse_ref, finish):
    rows = pl.ds(PAD, ROWS)

    def body(t, carry):
        for i in range(1, PLANES + 2, GROUP):
            magnetic = magnetic_planes(f, factor_ref[...], i) if i <= PLANES else []
            electric = electric_planes(f, inverse_ref, i - GROUP) if i > 1 else []
            for k, fields in enumerate(magnetic):
                for part, value in enumerate(fields):
                    f[3 + part, i + k, :, rows, :] = value
            for k, (ex, ey, ez) in enumerate(electric):
                j = i - GROUP + k
                f[0, j, :, rows, :] = ex
                f[1, j, :, rows, :] = ey
                f[2, j, :, rows, :] = finish(t, j, ez)
        return carry

    lax.fori_loop(0, STEPS, body, 0)


def entry_row(vector):
    whole = vector.astype(jnp.int32)
    return jnp.concatenate([whole[i : i + 1] for i in range(SUB)], axis=1)


def one_hot(rows, index):
    ids = lax.broadcasted_iota(jnp.int32, (rows, index.shape[1]), 0)
    return jnp.where(ids == index, 1.0, 0.0).astype(BF16)


def split(values):
    high = values.astype(BF16)
    return high, (values - high.astype(F32)).astype(BF16)


def write_back(f, outs):
    me = lax.axis_index("xy")
    for m, out in enumerate(outs):
        base = (me ^ m) * CX + 1
        for part in range(6):
            for x in range(CX):
                for zt in range(ZT):
                    out[(part * CX + x) * ZT + zt] = f[
                        part, base + x, 0, pl.ds(PAD + HALO + zt * SUB, SUB), :
                    ]


def clear_edges(f):
    for part in range(6):
        for plane in (0, PLANES + 1):
            f[part, plane] = jnp.zeros(f.shape[2:], F32)
        for start in (0, PAD + ROWS):
            f[part, :, :, pl.ds(start, PAD), :] = jnp.zeros((PLANES + 2, 2, PAD, LANES), F32)


def field_put(f, base):
    def put(part, x, row, columns, margins):
        plane = base + x
        rows = pl.ds(pl.multiple_of(PAD + row, SUB), SUB)
        f[part, plane, 0, rows, :] = columns
        f[part, plane, 1, rows, :] = margins

    return put


def forward_kernel(
    b0, b1, b2, b3, first_ref, second_ref, kernel_ref, token_ref,
    o0, o1, o2, o3, inverse_ref, table_ref,
    f, factor_ref, record_ref, picked_ref,
):
    me = lax.axis_index("xy")
    blocks = (b0, b1, b2, b3)
    clear_edges(f)
    row_first, row_second = edge_rows()
    size = packed_rows(7)
    for m, block in enumerate(blocks):
        base = (me ^ m) * CX + 1
        put_field = field_put(f, base)

        def put(part, x, row, columns, margins, base=base, put_field=put_field):
            if part == 6:
                inverse_ref[base + x, 0, pl.ds(row, SUB), :] = columns
                inverse_ref[base + x, 1, pl.ds(row, SUB), :] = margins
            else:
                put_field(part, x, row, columns, margins)

        sources = [
            (first_ref, m * size, row_first),
            (second_ref, m * size, row_second),
            (block, 0, HALO),
            (block, size, HALO + SUB),
        ]
        unpack(7, sources, put)
    factor_ref[...] = magnetic_factor()

    def finish(t, i, ez):
        x = i - 1
        for part, value in enumerate(split(ez[0, HALO : HALO + CZ])):
            record_ref[x // CX, part, t, x % CX] = value
        return ez

    run_steps(f, factor_ref, inverse_ref, finish)
    write_back(f, (o0, o1, o2, o3))

    bins = table_ref.shape[1]
    per_tile = CX * CZ
    copies = 2 * STEPS
    lists = ZT * packed_rows(7)
    bin_hots = []
    for m, block in enumerate(blocks):
        cells = entry_row(block[lists])
        where = jnp.where((cells // LANES) % TILES == me, cells // (LANES * TILES), -1)
        bin_hots.append(one_hot(bins, entry_row(block[lists + 1])))
        values = record_ref[me ^ m].reshape(copies * per_tile, LANES)
        for start in range(0, ENTRIES, CHUNK):
            span = slice(start, start + CHUNK)
            lane_hot = one_hot(LANES, cells[:, span] % LANES)
            row_ids = lax.broadcasted_iota(jnp.int32, (per_tile, CHUNK), 0)
            hit = row_ids == where[:, span]
            at_lane = jnp.dot(values, lane_hot, preferred_element_type=F32)
            at_lane = at_lane.reshape(copies, per_tile, CHUNK)
            picked = jnp.where(hit[None], at_lane, 0.0).astype(BF16)
            picked_ref[:, m * ENTRIES + start : m * ENTRIES + start + CHUNK] = picked.reshape(
                copies * per_tile, CHUNK
            )
    sums = lax.dot_general(
        picked_ref[...],
        jnp.concatenate(bin_hots, axis=1),
        (((1,), (1,)), ((), ())),
        preferred_element_type=F32,
    )
    table_ref[...] = jnp.dot(
        kernel_ref[...], sums, precision=lax.Precision.HIGHEST, preferred_element_type=F32
    )


def adjoint_kernel(
    b0, b1, b2, b3, first_ref, second_ref, inverse_ref, totals_ref, weight_ref, kernel_ref,
    o0, o1, o2, o3,
    f, factor_ref, drive_ref,
):
    me = lax.axis_index("xy")
    even = lax.rem(lax.axis_index("gz"), 2) == 0
    blocks = (b0, b1, b2, b3)
    clear_edges(f)
    row_first, row_second = edge_rows()
    size = packed_rows(6)
    for m, block in enumerate(blocks):
        sources = [
            (first_ref, m * (size + 2), row_first),
            (second_ref, m * (size + 2), row_second),
            (block, 0, HALO),
            (block, size, HALO + SUB),
        ]
        unpack(6, sources, field_put(f, (me ^ m) * CX + 1))
    factor_ref[...] = magnetic_factor()

    totals = totals_ref[...]
    bins = totals.shape[1]
    coefficients = normalize(totals, weight_ref[...])
    by_bin = jnp.zeros((STEPS, bins), F32)
    for k in range(2 * NFREQ):
        by_bin = by_bin + kernel_ref[:, k : k + 1] * coefficients[k : k + 1, :]
    by_bin = jnp.concatenate(split(by_bin), axis=0)

    def drive(ref, start, planes, z_first, z_count, row):
        cells = entry_row(ref[start]) - 1
        bin_hot = one_hot(bins, entry_row(ref[start + 1]))
        columns = cells % (LANES * TILES) - me * LANES
        inside = jnp.logical_and(columns >= -HALO, columns < LANES + HALO)
        inside = jnp.logical_and(inside, cells >= 0)
        lane_hot = one_hot(WIDE, jnp.where(inside, columns % WIDE, -1))
        z = (cells // (LANES * TILES)) % CZ - z_first
        x = cells // (LANES * TILES * CZ)
        kept = jnp.logical_and(z >= 0, z < z_count)
        where = jnp.where(kept, x * z_count + z, -1)
        count = CX * z_count
        hit = lax.broadcasted_iota(jnp.int32, (count, ENTRIES), 0) == where
        amplitude = jnp.dot(by_bin, bin_hot, preferred_element_type=F32)
        spread = jnp.concatenate(
            [
                jnp.where(hit, amplitude[k : k + 1, :], 0.0).astype(BF16)
                for k in range(2 * STEPS)
            ],
            axis=0,
        )
        total = lax.dot_general(
            spread, lane_hot, (((1,), (1,)), ((), ())), preferred_element_type=F32
        )
        total = total[: STEPS * count] + total[STEPS * count :]
        for t in range(STEPS):
            for k in range(CX):
                at = t * count + k * z_count
                for half in range(2):
                    drive_ref[t, planes + k, half, pl.ds(row, z_count), :] = total[
                        at : at + z_count, half * LANES : (half + 1) * LANES
                    ]

    z_first = jnp.where(even, 0, HALO)
    for m, block in enumerate(blocks):
        planes = (me ^ m) * CX
        base = m * (size + 2) + size
        drive(block, ZT * size, planes, 0, CZ, HALO)
        drive(first_ref, base, planes, z_first, HALO, row_first)
        drive(second_ref, base, planes, HALO - z_first, HALO, row_second)

    run_steps(f, factor_ref, inverse_ref, lambda t, i, ez: ez + drive_ref[t, i - 1])
    write_back(f, (o0, o1, o2, o3))


def spread_kernel(b0, b1, b2, b3, out_ref):
    me = lax.axis_index("xy")
    for m, block in enumerate((b0, b1, b2, b3)):
        lane = pl.multiple_of((me ^ m) * LANES, LANES)
        for part in range(6):
            for x in range(CX):
                for zt in range(ZT):
                    out_ref[part, x, zt * SUB : (zt + 1) * SUB, pl.ds(lane, LANES)] = block[
                        (part * CX + x) * ZT + zt
                    ]


def struct(*shape):
    return jax.ShapeDtypeStruct(shape, F32)


def call(kernel, args, outs, scratch=(), places=None, limit=48 * 1024 * 1024):
    spaces = places or {}
    return pl.pallas_call(
        kernel,
        out_shape=outs,
        in_specs=[
            pl.BlockSpec(memory_space=spaces.get(k, pltpu.VMEM)) for k in range(len(args))
        ],
        out_specs=jax.tree.map(lambda _: pl.BlockSpec(memory_space=pltpu.VMEM), outs),
        scratch_shapes=list(scratch),
        compiler_params=pltpu.CompilerParams(vmem_limit_bytes=limit),
    )(*args)


def swap(value, axis, distance):
    count = lax.axis_size(axis)
    return lax.ppermute(value, axis, [(i, i ^ distance) for i in range(count)])


def swap_blocks(blocks):
    return [blocks[0]] + [swap(blocks[m], "xy", m) for m in range(1, TILES)]


def swap_neighbours(first, second):
    count = lax.axis_size("gz")
    pairs = [(i, i ^ 1) for i in range(count) if i ^ 1 < count]
    others = [(i, ((i + 1) ^ 1) - 1) for i in range(count)]
    others = [(i, j) for i, j in others if 0 <= j < count]
    return lax.ppermute(first, "gz", pairs), lax.ppermute(second, "gz", others)


def sum_over(table, axis):
    terms = [table] + [swap(table, axis, m) for m in range(1, lax.axis_size(axis))]
    while len(terms) > 1:
        terms = [a + b for a, b in zip(terms[::2], terms[1::2])]
    return terms[0]


def local_columns(
    fields,
    adjoint_fields,
    material_ids,
    material_eps,
    monitor_cells,
    monitor_bins,
    source_cells,
    source_bins,
    bin_weight,
):
    bins = bin_weight.shape[0]
    record_kernel, source_kernel = time_kernels(STEPS)
    by_row = np.tile(np.repeat(record_kernel.T, CX * CZ, axis=1), (1, 2))
    n_fwd, n_adj = packed_rows(7), packed_rows(6)
    hbm = pltpu.HBM
    listed = pltpu.VMEM(monitor_cells.shape, jnp.int32)
    sent = call(
        pack_forward_kernel,
        (fields, material_ids, material_eps, monitor_cells, monitor_bins),
        [struct(ZT * n_fwd + 2, SUB, LANES)] * TILES,
        [
            pltpu.VMEM(fields.shape, F32),
            pltpu.VMEM(material_ids.shape, jnp.int32),
            pltpu.SMEM(material_eps.shape, F32),
            listed,
            listed,
            pltpu.VMEM(material_ids.shape, F32),
            pltpu.SemaphoreType.DMA((5,)),
        ],
        places={k: hbm for k in range(5)},
        limit=None,
    )
    *adjoint_sent, weight, back_kernel = call(
        pack_adjoint_kernel,
        (adjoint_fields, source_cells, source_bins, bin_weight.reshape(1, bins), source_kernel),
        [struct(ZT * n_adj + 2, SUB, LANES)] * TILES
        + [struct(1, bins), struct(STEPS, 2 * NFREQ)],
        [pltpu.VMEM(fields.shape, F32), listed, listed, pltpu.SemaphoreType.DMA((3,))],
        places={k: hbm for k in range(3)},
        limit=None,
    )
    blocks = swap_blocks(sent)
    slabs = call(
        functools.partial(slab_kernel, 7, 0), blocks, [struct(TILES * n_fwd, SUB, LANES)] * 2
    )
    first, second = swap_neighbours(*slabs)
    adjoint_blocks = swap_blocks(adjoint_sent)
    adjoint_slabs = call(
        functools.partial(slab_kernel, 6, 2),
        adjoint_blocks,
        [struct(TILES * (n_adj + 2), SUB, LANES)] * 2,
    )
    adjoint_edges = swap_neighbours(*adjoint_slabs)
    token = swap(adjoint_slabs[0], "xy", 1)
    field = pltpu.VMEM((6, PLANES + 2, 2, ROWS + 2 * PAD, LANES), F32)
    factor = pltpu.VMEM((2, ROWS, LANES), F32)
    *forward_sent, inverse, table = call(
        forward_kernel,
        (*blocks, first, second, by_row, token),
        [struct(6 * CX * ZT, SUB, LANES)] * TILES
        + [struct(PLANES + 2, 2, ROWS, LANES), struct(2 * NFREQ, bins)],
        [
            field,
            factor,
            pltpu.VMEM((TILES, 2, STEPS, CX, CZ, LANES), BF16),
            pltpu.VMEM((2 * STEPS * CX * CZ, TILES * ENTRIES), BF16),
        ],
        places={7: hbm},
    )
    table, forward_sent = lax.optimization_barrier((sum_over(table, "xy"), forward_sent))
    totals = sum_over(table, "gz")
    forward_blocks = swap_blocks(forward_sent)
    own_count = bins // (lax.axis_size("xy") * lax.axis_size("gz"))
    device_rank = lax.axis_index(("xy", "gz"))
    monitor_dft = lax.dynamic_slice_in_dim(totals, device_rank * own_count, own_count, axis=1)
    adjoint_back = call(
        adjoint_kernel,
        (
            *adjoint_blocks,
            *adjoint_edges,
            inverse,
            totals,
            weight,
            back_kernel,
        ),
        [struct(6 * CX * ZT, SUB, LANES)] * TILES,
        [field, factor, pltpu.VMEM((STEPS, PLANES, 2, ROWS, LANES), F32)],
    )
    forward_out = call(spread_kernel, forward_blocks, struct(*fields.shape))
    adjoint_out = call(spread_kernel, swap_blocks(adjoint_back), struct(*fields.shape))
    return (forward_out, adjoint_out, monitor_dft)


def solution(mesh):
    placed = (
        P("grp", "xy", "gz", None),
        P("grp", "xy", "gz", None),
        P("xy", "gz", "grp"),
        P(),
        P("xy", "gz", "grp"),
        P("xy", "gz", "grp"),
        P("xy", "gz", "grp"),
        P("xy", "gz", "grp"),
        P("grp"),
    )
    columns = mesh.shape["xy"] == TILES and mesh.shape["gz"] & (mesh.shape["gz"] - 1) == 0
    return jax.shard_map(
        local_columns if columns else local_general,
        mesh=mesh,
        in_specs=placed,
        out_specs=(P("grp", "xy", "gz", None), P("grp", "xy", "gz", None), P("grp", ("xy", "gz"))),
        check_vma=False,
    )
```

```python
import functools

import jax
import jax.numpy as jnp
import numpy as np
from jax import lax
from jax.experimental import pallas as pl
from jax.experimental.pallas import tpu as pltpu
from jax.sharding import PartitionSpec as P

STEPS = 8
NFREQ = 4
STEP_RATIO = 0.5


def from_behind(value, axis, steps):
    count = lax.axis_size(axis)
    first, last = (max(0, -steps), min(count, count - steps))
    return lax.ppermute(value, axis, [(source, source + steps) for source in range(first, last)])


def forward_diff(values, after, along):
    upper = jnp.concatenate(
        [
            lax.slice_in_dim(values, 1, values.shape[along], axis=along),
            jnp.expand_dims(after, along),
        ],
        axis=along,
    )
    return upper - values


def backward_diff(values, before, along):
    lower = jnp.concatenate(
        [
            jnp.expand_dims(before, along),
            lax.slice_in_dim(values, 0, values.shape[along] - 1, axis=along),
        ],
        axis=along,
    )
    return values - lower


def update_magnetic(electric, magnetic):
    electric_x, electric_y, electric_z = electric
    magnetic_x, magnetic_y, magnetic_z = magnetic
    x_next = from_behind(jnp.stack([electric_y[0], electric_z[0]]), "xy", -1)
    z_next = from_behind(jnp.stack([electric_x[:, 0], electric_y[:, 0]]), "gz", -1)
    zero_y = jnp.zeros_like(electric_x[:, :, 0])
    magnetic_x = magnetic_x - STEP_RATIO * (
        forward_diff(electric_z, zero_y, 2) - forward_diff(electric_y, z_next[1], 1)
    )
    magnetic_y = magnetic_y - STEP_RATIO * (
        forward_diff(electric_x, z_next[0], 1) - forward_diff(electric_z, x_next[1], 0)
    )
    magnetic_z = magnetic_z - STEP_RATIO * (
        forward_diff(electric_y, x_next[0], 0) - forward_diff(electric_x, zero_y, 2)
    )
    return (magnetic_x, magnetic_y, magnetic_z)


def update_electric(electric, magnetic, inverse):
    electric_x, electric_y, electric_z = electric
    magnetic_x, magnetic_y, magnetic_z = magnetic
    x_prev = from_behind(jnp.stack([magnetic_y[-1], magnetic_z[-1]]), "xy", 1)
    z_prev = from_behind(jnp.stack([magnetic_x[:, -1], magnetic_y[:, -1]]), "gz", 1)
    zero_y = jnp.zeros_like(electric_x[:, :, 0])
    electric_x = electric_x + STEP_RATIO * inverse * (
        backward_diff(magnetic_z, zero_y, 2) - backward_diff(magnetic_y, z_prev[1], 1)
    )
    electric_y = electric_y + STEP_RATIO * inverse * (
        backward_diff(magnetic_x, z_prev[0], 1) - backward_diff(magnetic_z, x_prev[1], 0)
    )
    electric_z = electric_z + STEP_RATIO * inverse * (
        backward_diff(magnetic_y, x_prev[0], 0) - backward_diff(magnetic_x, zero_y, 2)
    )
    return (electric_x, electric_y, electric_z)


def inverse_permittivity(material_ids, material_eps):
    result = jnp.zeros(material_ids.shape, jnp.float32)
    for material in range(material_eps.shape[0]):
        result = jnp.where(material_ids == material, 1.0 / material_eps[material], result)
    return result


def time_kernels(count):
    times = np.arange(count) + 1.0
    omegas = 0.3 + 0.35 * np.arange(NFREQ)
    phases = times[:, None] * omegas[None, :]
    record_kernel = np.concatenate([np.cos(phases), -np.sin(phases)], axis=1)
    reverse = count - np.arange(count)
    back_phases = reverse[:, None] * omegas[None, :]
    source_kernel = np.concatenate([np.cos(back_phases), np.sin(back_phases)], axis=1)
    return (record_kernel.astype(np.float32), source_kernel.astype(np.float32))


def normalize(totals, weights):
    real_part = totals[:NFREQ]
    imag_part = totals[NFREQ:]
    scale = weights / jnp.sqrt(1.0 + real_part * real_part + imag_part * imag_part)
    return jnp.concatenate([real_part * scale, imag_part * scale], axis=0)


def local_general(
    fields,
    adjoint_fields,
    material_ids,
    material_eps,
    monitor_cells,
    monitor_bins,
    source_cells,
    source_bins,
    bin_weight,
):
    inverse = inverse_permittivity(material_ids, material_eps)
    record_kernel, source_kernel = time_kernels(STEPS)
    watched = monitor_cells.reshape(-1)
    electric = (fields[0], fields[1], fields[2])
    magnetic = (fields[3], fields[4], fields[5])
    records = []
    for _ in range(STEPS):
        magnetic = update_magnetic(electric, magnetic)
        electric = update_electric(electric, magnetic, inverse)
        records.append(electric[2].reshape(-1)[watched])
    forward_out = jnp.stack(list(electric) + list(magnetic))
    samples = jnp.stack(records)
    partial_dft = jnp.dot(samples.T, record_kernel, precision=lax.Precision.HIGHEST)
    bin_table = jax.ops.segment_sum(
        partial_dft, monitor_bins.reshape(-1), num_segments=bin_weight.shape[0]
    ).T
    owners = lax.axis_size("xy") * lax.axis_size("gz")
    own_count = bin_table.shape[1] // owners
    device_rank = lax.axis_index(("xy", "gz"))
    totals = lax.psum(bin_table, ("xy", "gz"))
    monitor_dft = lax.dynamic_slice_in_dim(totals, device_rank * own_count, own_count, axis=1)
    coefficients = normalize(totals, bin_weight[None, :])
    picked = jnp.take(coefficients, source_bins.reshape(-1), axis=1)
    amplitudes = jnp.dot(source_kernel, picked, precision=lax.Precision.HIGHEST)
    targets = source_cells.reshape(-1)
    electric = (adjoint_fields[0], adjoint_fields[1], adjoint_fields[2])
    magnetic = (adjoint_fields[3], adjoint_fields[4], adjoint_fields[5])
    for step_index in range(STEPS):
        magnetic = update_magnetic(electric, magnetic)
        electric = update_electric(electric, magnetic, inverse)
        driven = (
            electric[2]
            .reshape(-1)
            .at[targets]
            .add(amplitudes[step_index])
            .reshape(electric[2].shape)
        )
        electric = (electric[0], electric[1], driven)
    adjoint_out = jnp.stack(list(electric) + list(magnetic))
    return (forward_out, adjoint_out, monitor_dft)


TILES = 4
CX = 4
CZ = 16
LANES = 128
HALO = 8
ROWS = CZ + 2 * HALO
PAD = 8
GROUP = 4
WIDE = 2 * LANES
PLANES = TILES * CX
ENTRIES = 1024
CHUNK = 256
SUB = 8
ZT = CZ // SUB
BF16 = jnp.bfloat16
F32 = jnp.float32


def packed_rows(parts):
    return parts * CX + (parts + 1) // 2


def lane_ids():
    return lax.broadcasted_iota(jnp.int32, (SUB, LANES), 1)


def pack_block(read, regions, parts, column, store):
    lanes = lane_ids()
    upper = lanes >= LANES // 2
    take_left = jnp.logical_and(upper, column > 0)
    take_right = jnp.logical_and(jnp.logical_not(upper), column < TILES - 1)
    here = pl.multiple_of(column * LANES, LANES)
    left = pl.multiple_of(jnp.maximum(column - 1, 0) * LANES, LANES)
    right = pl.multiple_of(jnp.minimum(column + 1, TILES - 1) * LANES, LANES)
    size = packed_rows(parts)
    for zt in range(regions):
        margins = [jnp.zeros((SUB, LANES), F32) for _ in range((parts + 1) // 2)]
        for part in range(parts):
            for x in range(CX):
                store(zt * size + part * CX + x, read(part, x, zt, here))
                both = jnp.where(
                    take_left,
                    read(part, x, zt, left),
                    jnp.where(take_right, read(part, x, zt, right), 0.0),
                )
                slot = (part % 2) * CX + x
                placed = pltpu.roll(both, (16 * slot + HALO) % LANES, 1)
                margins[part // 2] = jnp.where(lanes // 16 == slot, placed, margins[part // 2])
        for pair, margin in enumerate(margins):
            store(zt * size + parts * CX + pair, margin)


def fetch(pairs, sems):
    copies = [
        pltpu.make_async_copy(source, target, sems.at[k])
        for k, (source, target) in enumerate(pairs)
    ]
    for copy in copies:
        copy.start()
    for copy in copies:
        copy.wait()


def put_list(out, row, lanes, list_ref, offset):
    for i in range(SUB):
        entries = list_ref[0, :, i * LANES : (i + 1) * LANES]
        out[row, i : i + 1, lanes] = (entries + offset).astype(F32)


def pack_forward_kernel(
    fields_hbm, ids_hbm, eps_hbm, cells_hbm, bins_hbm,
    o0, o1, o2, o3,
    fields_ref, ids_ref, eps_ref, cells_ref, bins_ref, inverse_ref, sems,
):
    me = lax.axis_index("xy")
    fetch(
        [
            (fields_hbm, fields_ref),
            (ids_hbm, ids_ref),
            (eps_hbm, eps_ref),
            (cells_hbm, cells_ref),
            (bins_hbm, bins_ref),
        ],
        sems,
    )
    ids = ids_ref[...]
    eps = jnp.full(ids.shape, eps_ref[0], F32)
    for material in range(1, eps_ref.shape[0]):
        eps = jnp.where(ids == material, eps_ref[material], eps)
    inverse_ref[...] = STEP_RATIO * (1.0 / eps)

    def read(part, x, zt, lane):
        rows = pl.ds(zt * SUB, SUB)
        if part == 6:
            return inverse_ref[x, rows, pl.ds(lane, LANES)]
        return fields_ref[part, x, rows, pl.ds(lane, LANES)]

    for m, out in enumerate((o0, o1, o2, o3)):

        def store(row, value, out=out):
            out[row] = value

        pack_block(read, ZT, 7, me ^ m, store)
        for k, ref in enumerate((cells_ref, bins_ref)):
            put_list(out, ZT * packed_rows(7) + k, slice(0, LANES), ref, 0)


def pack_adjoint_kernel(
    fields_hbm, cells_hbm, bins_hbm, weight_ref, kernel_ref,
    o0, o1, o2, o3, weight_out, kernel_out,
    fields_ref, cells_ref, bins_ref, sems,
):
    me = lax.axis_index("xy")
    fetch([(fields_hbm, fields_ref), (cells_hbm, cells_ref), (bins_hbm, bins_ref)], sems)
    weight_out[...] = weight_ref[...]
    kernel_out[...] = kernel_ref[...]

    def read(part, x, zt, lane):
        return fields_ref[part, x, pl.ds(zt * SUB, SUB), pl.ds(lane, LANES)]

    for m, out in enumerate((o0, o1, o2, o3)):

        def store(row, value, out=out):
            out[row] = value

        pack_block(read, ZT, 6, me ^ m, store)
        put_list(out, ZT * packed_rows(6), slice(0, LANES), cells_ref, 1)
        put_list(out, ZT * packed_rows(6) + 1, slice(0, LANES), bins_ref, 0)


def slab_kernel(parts, lists, b0, b1, b2, b3, first_ref, second_ref):
    size = packed_rows(parts)
    zt_first = jnp.where(lax.rem(lax.axis_index("gz"), 2) == 0, 1, 0)
    for m, block in enumerate((b0, b1, b2, b3)):
        base = m * (size + lists)
        first_ref[pl.ds(base, size)] = block[pl.ds(zt_first * size, size)]
        second_ref[pl.ds(base, size)] = block[pl.ds((1 - zt_first) * size, size)]
        for k in range(lists):
            first_ref[base + size + k] = block[ZT * size + k]
            second_ref[base + size + k] = block[ZT * size + k]


def edge_rows():
    even = lax.rem(lax.axis_index("gz"), 2) == 0
    return (
        pl.multiple_of(jnp.where(even, HALO + CZ, 0), SUB),
        pl.multiple_of(jnp.where(even, 0, HALO + CZ), SUB),
    )


def unpack(parts, sources, put):
    lanes = lane_ids()
    in_margin = jnp.logical_or(lanes < HALO, lanes >= LANES - HALO)
    for ref, start, row in sources:
        for part in range(parts):
            for x in range(CX):
                slot = (part % 2) * CX + x
                margin = pltpu.roll(
                    ref[start + parts * CX + part // 2], (-16 * slot - HALO) % LANES, 1
                )
                put(
                    part,
                    x,
                    row,
                    ref[start + part * CX + x],
                    jnp.where(in_margin, margin, 0.0),
                )


def magnetic_factor():
    halves = lax.broadcasted_iota(jnp.int32, (2, ROWS, LANES), 0)
    rows = lax.broadcasted_iota(jnp.int32, (2, ROWS, LANES), 1)
    lanes = lax.broadcasted_iota(jnp.int32, (2, ROWS, LANES), 2)
    below_z = jnp.logical_and(rows < HALO, lax.axis_index("gz") == 0)
    below_y = jnp.logical_and(halves == 1, lanes >= LANES - HALO)
    below_y = jnp.logical_and(below_y, lax.axis_index("xy") == 0)
    return jnp.where(jnp.logical_or(below_z, below_y), 0.0, STEP_RATIO)


def y_up(v):
    moved = pltpu.roll(v, LANES - 1, 2)
    other = jnp.concatenate([moved[1:], moved[:1]], axis=0)
    lanes = lax.broadcasted_iota(jnp.int32, v.shape, 2)
    return jnp.where(lanes == LANES - 1, other, moved)


def y_down(v):
    moved = pltpu.roll(v, 1, 2)
    other = jnp.concatenate([moved[1:], moved[:1]], axis=0)
    lanes = lax.broadcasted_iota(jnp.int32, v.shape, 2)
    return jnp.where(lanes == 0, other, moved)


def magnetic_planes(f, factor, i):
    rows, above = pl.ds(PAD, ROWS), pl.ds(PAD + 1, ROWS)
    ey = [f[1, i + k, :, rows, :] for k in range(GROUP + 1)]
    ez = [f[2, i + k, :, rows, :] for k in range(GROUP + 1)]
    done = []
    for k in range(GROUP):
        ex, ex_up = f[0, i + k, :, rows, :], f[0, i + k, :, above, :]
        ey_up = f[1, i + k, :, above, :]
        hx = f[3, i + k, :, rows, :] - factor * ((y_up(ez[k]) - ez[k]) - (ey_up - ey[k]))
        hy = f[4, i + k, :, rows, :] - factor * ((ex_up - ex) - (ez[k + 1] - ez[k]))
        hz = f[5, i + k, :, rows, :] - factor * ((ey[k + 1] - ey[k]) - (y_up(ex) - ex))
        done.append((hx, hy, hz))
    return done


def electric_planes(f, inverse_ref, i):
    rows, below = pl.ds(PAD, ROWS), pl.ds(PAD - 1, ROWS)
    hy = [f[4, i - 1 + k, :, rows, :] for k in range(GROUP + 1)]
    hz = [f[5, i - 1 + k, :, rows, :] for k in range(GROUP + 1)]
    done = []
    for k in range(GROUP):
        hx, hx_down = f[3, i + k, :, rows, :], f[3, i + k, :, below, :]
        hy_down = f[4, i + k, :, below, :]
        y, z = hy[k + 1], hz[k + 1]
        inverse = inverse_ref[i + k]
        ex = f[0, i + k, :, rows, :] + inverse * ((z - y_down(z)) - (y - hy_down))
        ey = f[1, i + k, :, rows, :] + inverse * ((hx - hx_down) - (z - hz[k]))
        ez = f[2, i + k, :, rows, :] + inverse * ((y - hy[k]) - (hx - y_down(hx)))
        done.append((ex, ey, ez))
    return done


def run_steps(f, factor_ref, inverse_ref, finish):
    rows = pl.ds(PAD, ROWS)

    def body(t, carry):
        for i in range(1, PLANES + 2, GROUP):
            magnetic = magnetic_planes(f, factor_ref[...], i) if i <= PLANES else []
            electric = electric_planes(f, inverse_ref, i - GROUP) if i > 1 else []
            for k, fields in enumerate(magnetic):
                for part, value in enumerate(fields):
                    f[3 + part, i + k, :, rows, :] = value
            for k, (ex, ey, ez) in enumerate(electric):
                j = i - GROUP + k
                f[0, j, :, rows, :] = ex
                f[1, j, :, rows, :] = ey
                f[2, j, :, rows, :] = finish(t, j, ez)
        return carry

    lax.fori_loop(0, STEPS, body, 0)


def entry_row(vector):
    whole = vector.astype(jnp.int32)
    return jnp.concatenate([whole[i : i + 1] for i in range(SUB)], axis=1)


def one_hot(rows, index):
    ids = lax.broadcasted_iota(jnp.int32, (rows, index.shape[1]), 0)
    return jnp.where(ids == index, 1.0, 0.0).astype(BF16)


def split(values):
    high = values.astype(BF16)
    return high, (values - high.astype(F32)).astype(BF16)


def write_back(f, outs):
    me = lax.axis_index("xy")
    for m, out in enumerate(outs):
        base = (me ^ m) * CX + 1
        for part in range(6):
            for x in range(CX):
                for zt in range(ZT):
                    out[(part * CX + x) * ZT + zt] = f[
                        part, base + x, 0, pl.ds(PAD + HALO + zt * SUB, SUB), :
                    ]


def clear_edges(f):
    for part in range(6):
        for plane in (0, PLANES + 1):
            f[part, plane] = jnp.zeros(f.shape[2:], F32)
        for start in (0, PAD + ROWS):
            f[part, :, :, pl.ds(start, PAD), :] = jnp.zeros((PLANES + 2, 2, PAD, LANES), F32)


def field_put(f, base):
    def put(part, x, row, columns, margins):
        plane = base + x
        rows = pl.ds(pl.multiple_of(PAD + row, SUB), SUB)
        f[part, plane, 0, rows, :] = columns
        f[part, plane, 1, rows, :] = margins

    return put


def forward_kernel(
    b0, b1, b2, b3, first_ref, second_ref, kernel_ref, token_ref,
    o0, o1, o2, o3, inverse_ref, table_ref,
    f, factor_ref, record_ref, picked_ref,
):
    me = lax.axis_index("xy")
    blocks = (b0, b1, b2, b3)
    clear_edges(f)
    row_first, row_second = edge_rows()
    size = packed_rows(7)
    for m, block in enumerate(blocks):
        base = (me ^ m) * CX + 1
        put_field = field_put(f, base)

        def put(part, x, row, columns, margins, base=base, put_field=put_field):
            if part == 6:
                inverse_ref[base + x, 0, pl.ds(row, SUB), :] = columns
                inverse_ref[base + x, 1, pl.ds(row, SUB), :] = margins
            else:
                put_field(part, x, row, columns, margins)

        sources = [
            (first_ref, m * size, row_first),
            (second_ref, m * size, row_second),
            (block, 0, HALO),
            (block, size, HALO + SUB),
        ]
        unpack(7, sources, put)
    factor_ref[...] = magnetic_factor()

    def finish(t, i, ez):
        x = i - 1
        for part, value in enumerate(split(ez[0, HALO : HALO + CZ])):
            record_ref[x // CX, part, t, x % CX] = value
        return ez

    run_steps(f, factor_ref, inverse_ref, finish)
    write_back(f, (o0, o1, o2, o3))

    bins = table_ref.shape[1]
    per_tile = CX * CZ
    copies = 2 * STEPS
    lists = ZT * packed_rows(7)
    bin_hots = []
    for m, block in enumerate(blocks):
        cells = entry_row(block[lists])
        where = jnp.where((cells // LANES) % TILES == me, cells // (LANES * TILES), -1)
        bin_hots.append(one_hot(bins, entry_row(block[lists + 1])))
        values = record_ref[me ^ m].reshape(copies * per_tile, LANES)
        for start in range(0, ENTRIES, CHUNK):
            span = slice(start, start + CHUNK)
            lane_hot = one_hot(LANES, cells[:, span] % LANES)
            row_ids = lax.broadcasted_iota(jnp.int32, (per_tile, CHUNK), 0)
            hit = row_ids == where[:, span]
            at_lane = jnp.dot(values, lane_hot, preferred_element_type=F32)
            at_lane = at_lane.reshape(copies, per_tile, CHUNK)
            picked = jnp.where(hit[None], at_lane, 0.0).astype(BF16)
            picked_ref[:, m * ENTRIES + start : m * ENTRIES + start + CHUNK] = picked.reshape(
                copies * per_tile, CHUNK
            )
    sums = lax.dot_general(
        picked_ref[...],
        jnp.concatenate(bin_hots, axis=1),
        (((1,), (1,)), ((), ())),
        preferred_element_type=F32,
    )
    table_ref[...] = jnp.dot(
        kernel_ref[...], sums, precision=lax.Precision.HIGHEST, preferred_element_type=F32
    )


def adjoint_kernel(
    b0, b1, b2, b3, first_ref, second_ref, inverse_ref, totals_ref, weight_ref, kernel_ref,
    o0, o1, o2, o3,
    f, factor_ref, drive_ref,
):
    me = lax.axis_index("xy")
    even = lax.rem(lax.axis_index("gz"), 2) == 0
    blocks = (b0, b1, b2, b3)
    clear_edges(f)
    row_first, row_second = edge_rows()
    size = packed_rows(6)
    for m, block in enumerate(blocks):
        sources = [
            (first_ref, m * (size + 2), row_first),
            (second_ref, m * (size + 2), row_second),
            (block, 0, HALO),
            (block, size, HALO + SUB),
        ]
        unpack(6, sources, field_put(f, (me ^ m) * CX + 1))
    factor_ref[...] = magnetic_factor()

    totals = totals_ref[...]
    bins = totals.shape[1]
    coefficients = normalize(totals, weight_ref[...])
    by_bin = jnp.zeros((STEPS, bins), F32)
    for k in range(2 * NFREQ):
        by_bin = by_bin + kernel_ref[:, k : k + 1] * coefficients[k : k + 1, :]
    by_bin = jnp.concatenate(split(by_bin), axis=0)

    def drive(ref, start, planes, z_first, z_count, row):
        cells = entry_row(ref[start]) - 1
        bin_hot = one_hot(bins, entry_row(ref[start + 1]))
        columns = cells % (LANES * TILES) - me * LANES
        inside = jnp.logical_and(columns >= -HALO, columns < LANES + HALO)
        inside = jnp.logical_and(inside, cells >= 0)
        lane_hot = one_hot(WIDE, jnp.where(inside, columns % WIDE, -1))
        z = (cells // (LANES * TILES)) % CZ - z_first
        x = cells // (LANES * TILES * CZ)
        kept = jnp.logical_and(z >= 0, z < z_count)
        where = jnp.where(kept, x * z_count + z, -1)
        count = CX * z_count
        hit = lax.broadcasted_iota(jnp.int32, (count, ENTRIES), 0) == where
        amplitude = jnp.dot(by_bin, bin_hot, preferred_element_type=F32)
        spread = jnp.concatenate(
            [
                jnp.where(hit, amplitude[k : k + 1, :], 0.0).astype(BF16)
                for k in range(2 * STEPS)
            ],
            axis=0,
        )
        total = lax.dot_general(
            spread, lane_hot, (((1,), (1,)), ((), ())), preferred_element_type=F32
        )
        total = total[: STEPS * count] + total[STEPS * count :]
        for t in range(STEPS):
            for k in range(CX):
                at = t * count + k * z_count
                for half in range(2):
                    drive_ref[t, planes + k, half, pl.ds(row, z_count), :] = total[
                        at : at + z_count, half * LANES : (half + 1) * LANES
                    ]

    z_first = jnp.where(even, 0, HALO)
    for m, block in enumerate(blocks):
        planes = (me ^ m) * CX
        base = m * (size + 2) + size
        drive(block, ZT * size, planes, 0, CZ, HALO)
        drive(first_ref, base, planes, z_first, HALO, row_first)
        drive(second_ref, base, planes, HALO - z_first, HALO, row_second)

    run_steps(f, factor_ref, inverse_ref, lambda t, i, ez: ez + drive_ref[t, i - 1])
    write_back(f, (o0, o1, o2, o3))


def spread_kernel(b0, b1, b2, b3, out_ref):
    me = lax.axis_index("xy")
    for m, block in enumerate((b0, b1, b2, b3)):
        lane = pl.multiple_of((me ^ m) * LANES, LANES)
        for part in range(6):
            for x in range(CX):
                for zt in range(ZT):
                    out_ref[part, x, zt * SUB : (zt + 1) * SUB, pl.ds(lane, LANES)] = block[
                        (part * CX + x) * ZT + zt
                    ]


def struct(*shape):
    return jax.ShapeDtypeStruct(shape, F32)


def call(kernel, args, outs, scratch=(), places=None, limit=48 * 1024 * 1024):
    spaces = places or {}
    return pl.pallas_call(
        kernel,
        out_shape=outs,
        in_specs=[
            pl.BlockSpec(memory_space=spaces.get(k, pltpu.VMEM)) for k in range(len(args))
        ],
        out_specs=jax.tree.map(lambda _: pl.BlockSpec(memory_space=pltpu.VMEM), outs),
        scratch_shapes=list(scratch),
        compiler_params=pltpu.CompilerParams(vmem_limit_bytes=limit),
    )(*args)


def swap(value, axis, distance):
    count = lax.axis_size(axis)
    return lax.ppermute(value, axis, [(i, i ^ distance) for i in range(count)])


def swap_blocks(blocks):
    return [blocks[0]] + [swap(blocks[m], "xy", m) for m in range(1, TILES)]


def swap_neighbours(first, second):
    count = lax.axis_size("gz")
    pairs = [(i, i ^ 1) for i in range(count) if i ^ 1 < count]
    others = [(i, ((i + 1) ^ 1) - 1) for i in range(count)]
    others = [(i, j) for i, j in others if 0 <= j < count]
    return lax.ppermute(first, "gz", pairs), lax.ppermute(second, "gz", others)


def sum_over(table, axis):
    terms = [table] + [swap(table, axis, m) for m in range(1, lax.axis_size(axis))]
    while len(terms) > 1:
        terms = [a + b for a, b in zip(terms[::2], terms[1::2])]
    return terms[0]


def local_columns(
    fields,
    adjoint_fields,
    material_ids,
    material_eps,
    monitor_cells,
    monitor_bins,
    source_cells,
    source_bins,
    bin_weight,
):
    bins = bin_weight.shape[0]
    record_kernel, source_kernel = time_kernels(STEPS)
    by_row = np.tile(np.repeat(record_kernel.T, CX * CZ, axis=1), (1, 2))
    n_fwd, n_adj = packed_rows(7), packed_rows(6)
    hbm = pltpu.HBM
    listed = pltpu.VMEM(monitor_cells.shape, jnp.int32)
    sent = call(
        pack_forward_kernel,
        (fields, material_ids, material_eps, monitor_cells, monitor_bins),
        [struct(ZT * n_fwd + 2, SUB, LANES)] * TILES,
        [
            pltpu.VMEM(fields.shape, F32),
            pltpu.VMEM(material_ids.shape, jnp.int32),
            pltpu.SMEM(material_eps.shape, F32),
            listed,
            listed,
            pltpu.VMEM(material_ids.shape, F32),
            pltpu.SemaphoreType.DMA((5,)),
        ],
        places={k: hbm for k in range(5)},
        limit=None,
    )
    *adjoint_sent, weight, back_kernel = call(
        pack_adjoint_kernel,
        (adjoint_fields, source_cells, source_bins, bin_weight.reshape(1, bins), source_kernel),
        [struct(ZT * n_adj + 2, SUB, LANES)] * TILES
        + [struct(1, bins), struct(STEPS, 2 * NFREQ)],
        [pltpu.VMEM(fields.shape, F32), listed, listed, pltpu.SemaphoreType.DMA((3,))],
        places={k: hbm for k in range(3)},
        limit=None,
    )
    blocks = swap_blocks(sent)
    slabs = call(
        functools.partial(slab_kernel, 7, 0), blocks, [struct(TILES * n_fwd, SUB, LANES)] * 2
    )
    first, second = swap_neighbours(*slabs)
    adjoint_blocks = swap_blocks(adjoint_sent)
    adjoint_slabs = call(
        functools.partial(slab_kernel, 6, 2),
        adjoint_blocks,
        [struct(TILES * (n_adj + 2), SUB, LANES)] * 2,
    )
    adjoint_edges = swap_neighbours(*adjoint_slabs)
    token = swap(adjoint_slabs[0], "xy", 1)
    field = pltpu.VMEM((6, PLANES + 2, 2, ROWS + 2 * PAD, LANES), F32)
    factor = pltpu.VMEM((2, ROWS, LANES), F32)
    *forward_sent, inverse, table = call(
        forward_kernel,
        (*blocks, first, second, by_row, token),
        [struct(6 * CX * ZT, SUB, LANES)] * TILES
        + [struct(PLANES + 2, 2, ROWS, LANES), struct(2 * NFREQ, bins)],
        [
            field,
            factor,
            pltpu.VMEM((TILES, 2, STEPS, CX, CZ, LANES), BF16),
            pltpu.VMEM((2 * STEPS * CX * CZ, TILES * ENTRIES), BF16),
        ],
        places={7: hbm},
    )
    table, forward_sent = lax.optimization_barrier((sum_over(table, "xy"), forward_sent))
    totals = sum_over(table, "gz")
    forward_blocks = swap_blocks(forward_sent)
    own_count = bins // (lax.axis_size("xy") * lax.axis_size("gz"))
    device_rank = lax.axis_index(("xy", "gz"))
    monitor_dft = lax.dynamic_slice_in_dim(totals, device_rank * own_count, own_count, axis=1)
    adjoint_back = call(
        adjoint_kernel,
        (
            *adjoint_blocks,
            *adjoint_edges,
            inverse,
            totals,
            weight,
            back_kernel,
        ),
        [struct(6 * CX * ZT, SUB, LANES)] * TILES,
        [field, factor, pltpu.VMEM((STEPS, PLANES, 2, ROWS, LANES), F32)],
    )
    forward_out = call(spread_kernel, forward_blocks, struct(*fields.shape))
    adjoint_out = call(spread_kernel, swap_blocks(adjoint_back), struct(*fields.shape))
    return (forward_out, adjoint_out, monitor_dft)


def solution(mesh):
    placed = (
        P("grp", "xy", "gz", None),
        P("grp", "xy", "gz", None),
        P("xy", "gz", "grp"),
        P(),
        P("xy", "gz", "grp"),
        P("xy", "gz", "grp"),
        P("xy", "gz", "grp"),
        P("xy", "gz", "grp"),
        P("grp"),
    )
    columns = mesh.shape["xy"] == TILES and mesh.shape["gz"] & (mesh.shape["gz"] - 1) == 0
    return jax.shard_map(
        local_columns if columns else local_general,
        mesh=mesh,
        in_specs=placed,
        out_specs=(P("grp", "xy", "gz", None), P("grp", "xy", "gz", None), P("grp", ("xy", "gz"))),
        check_vma=False,
    )
```
